1024 devices in a mesh: fsdp: 16 (over y, x), tp: 8 (over z_hi, core), ad: 8 (over z_lo).
Axes of the slice: x: 4, y: 4, z: 32 (z_hi: 4, z_lo: 8; z = z_hi * 8 + z_lo), core: 2. Of those that a mesh axis runs over, the one named last changes fastest.
Arguments:
- input_rows: bfloat16 [32768, 8192], P(('fsdp', 'ad')), may hold values from -6 to 6
- value_weight_frozen: bfloat16 [8192, 1024], P('fsdp', 'tp'), may hold values from -0.0625 to 0.0625
- adapter_down_weight: bfloat16 [32, 256, 8192], P('ad', None, 'tp'), may hold values from -0.0625 to 0.0625
- adapter_up_weight: bfloat16 [32, 256, 1024], P('ad', None, 'tp'), may hold values from -0.375 to 0.375
- layer_output_gradient: bfloat16 [32768, 1024], P(('fsdp', 'ad'), 'tp'), may hold values from -0.5 to 0.5
- domain: int32 [32768, 1], P(('fsdp', 'ad')), may hold values from 0 to 31; in each aligned block of 256 rows (0 to 255, 256 to 511, ...) at most 12 rows name the same one
Outputs:
- y_out: bfloat16 [32768, 1024], P(('fsdp', 'ad'), 'tp')
- grad_a: float32 [32, 256, 8192], P('ad', 'fsdp', 'tp')
- grad_b: float32 [32, 256, 1024], P('ad', 'fsdp', 'tp')
The draws below stay inside these ranges and needn't reach their ends.
Inputs may be any that keep to these rules, and one draw needn't show every extreme that they name: In each aligned block of 256 rows (the tokens of one fsdp and ad index) no domain is named by more than 12 tokens, a bound that some block reaches.
All inputs are finite; a program needn't handle non-finite values.
Results may differ from the reference program's by a relative error of at most 0.004.
Values may be sent and summed in bfloat16 or wider, within the bound.
A program may use at most 64 MiB of HBM per device.

```python
import math
import jax
import jax.numpy as jnp
import numpy as np
from jax import lax

MODEL_WIDTH = 8192
VALUE_WIDTH = 1024
ADAPTER_RANK = 256
DOMAIN_COUNT = 32
TOK_GRP = 256
CAPD = 12
FSDP_ROWS = 2048
TOKENS = 32768
N_FSDP = 16
N_AD = 8


def levels(stream_key, shape, cuts, smallest, top_value):
    loudness, own = 1.0, jax.random.fold_in(stream_key, 6)
    for dim, blocks in cuts:
        steps = jnp.exp(jax.random.uniform(jax.random.fold_in(own, dim), (blocks,), jnp.float32, smallest / len(cuts), top_value / len(cuts)))
        loudness = loudness * jnp.repeat(steps, shape[dim] // blocks).reshape([-1 if axis == dim else 1 for axis in range(len(shape))])
    return loudness


def shared_out(rng, own, number, rows, count, top, bound, skew):
    order = jax.random.permutation(rng, count)
    packed, usual = load_shares(count, rows * top, bound, skew, True), load_shares(count, rows * top, bound, skew, False)
    places = jnp.arange(count)

    def named(lengths, turn):
        used = int((lengths > 0).sum())
        fixed = max(1, used // 4)
        moved = fixed + (places - fixed + turn * (used - fixed)) % max(1, count - fixed)
        return jnp.zeros((count,), jnp.int32).at[order[jnp.where(places < fixed, places, moved)]].set(jnp.asarray(lengths, jnp.int32))

    lengths = jnp.where(number % 4 == 0, named(packed, number // 4), named(usual, number - number // 4 - 1))
    mixed = jax.random.permutation(jax.random.fold_in(own, 3), count)
    giver, receiver = mixed[0:count // 2 * 2:2], mixed[1:count // 2 * 2:2]
    room = jnp.minimum(lengths[giver] - 1, bound - lengths[receiver]) // 2
    room = jnp.where((giver == order[0]) | (receiver == order[0]) | (lengths[receiver] == 0), 0, jnp.maximum(room, 0))
    moved = jax.random.randint(jax.random.fold_in(own, 4), (count // 2,), 0, 1 << 20) % (room + 1)
    lengths = lengths.at[giver].add(-moved).at[receiver].add(moved)
    labels = jnp.searchsorted(jnp.cumsum(lengths), jnp.arange(rows * top), side="right").astype(jnp.int32)
    grid = labels.reshape(top, rows).T
    grid = grid[jax.random.permutation(jax.random.fold_in(own, 1), rows)]
    turn = jax.random.randint(jax.random.fold_in(own, 2), (rows, 1), 0, top)
    return jnp.take_along_axis(grid, (jnp.arange(top)[None, :] + turn) % top, axis=1)


def load_shares(count, total, reach, skew, full):
    loads = [(1 << 20) // math.isqrt(standing ** skew) + 1 for standing in range(1, count + 1)]
    largest = reach if full else min(reach, max(-(-total // count), total * loads[0] // sum(loads)))
    least = 1 if total - largest >= count - 1 else 0
    counts, surplus = [largest] + [least] * (count - 1), total - largest - least * (count - 1)
    while surplus > 0:
        candidates = [i for i in range(1, count) if counts[i] < largest] or [i for i in range(1, count) if counts[i] < reach]
        whole, left = sum([loads[i] for i in candidates]), surplus
        for i in candidates:
            more = min(reach - counts[i], max(1, left * loads[i] // whole), surplus)
            counts[i] = counts[i] + more
            surplus = surplus - more
    return np.array(counts)


def bell_draw(key, dims, width, most, cuts=(), kind=jnp.bfloat16):
    result = width * jax.random.normal(key, dims, jnp.float32)
    if cuts:
        result = result * levels(key, dims, cuts, -0.22, 0.18)
    return jnp.clip(result, -most, most).astype(kind)


def setup_inputs(seed: int = 0) -> dict:
    seeds = jax.random.split(jax.random.key(seed), 7)
    input_rows = bell_draw(seeds[0], (TOKENS, MODEL_WIDTH), 1.0, 6.0, ((0, 128),))
    value_weight_frozen = bell_draw(seeds[1], (MODEL_WIDTH, VALUE_WIDTH), MODEL_WIDTH ** -0.5, 0.0625, ((0, 16), (1, 8)))
    adapter_down_weight = bell_draw(seeds[2], (DOMAIN_COUNT, ADAPTER_RANK, MODEL_WIDTH), MODEL_WIDTH ** -0.5, 0.0625, ((0, 8), (2, 8)))
    adapter_up_weight = bell_draw(seeds[3], (DOMAIN_COUNT, ADAPTER_RANK, VALUE_WIDTH), ADAPTER_RANK ** -0.5, 0.375, ((0, 8), (2, 8)))
    layer_output_gradient = bell_draw(seeds[4], (TOKENS, VALUE_WIDTH), 0.0625, 0.5, ((0, 128), (1, 8)))
    domain_keys = jax.random.split(jax.random.fold_in(seeds[5], 1), TOKENS // TOK_GRP)
    domain_turns = jax.random.permutation(jax.random.fold_in(seeds[5], 3), TOKENS // TOK_GRP)
    domain = jax.vmap(lambda own, number: shared_out(jax.random.fold_in(seeds[5], 2), own, number, TOK_GRP, DOMAIN_COUNT, 1, CAPD, 2))(domain_keys, domain_turns).reshape((TOKENS, 1))
    return dict(input_rows=input_rows, value_weight_frozen=value_weight_frozen, adapter_down_weight=adapter_down_weight, adapter_up_weight=adapter_up_weight, layer_output_gradient=layer_output_gradient, domain=domain)


adapter_scale = 0.5


def reference(input_rows, value_weight_frozen, adapter_down_weight, adapter_up_weight, layer_output_gradient, domain):
    slot_count = N_AD * CAPD
    down_weight_full = adapter_down_weight.astype(jnp.float32)
    up_weight_full = adapter_up_weight.astype(jnp.float32)
    x_blocks = input_rows.reshape(N_FSDP, FSDP_ROWS, MODEL_WIDTH)
    dy_blocks = layer_output_gradient.reshape(N_FSDP, FSDP_ROWS, VALUE_WIDTH)
    dom_blocks = domain[:, 0].reshape(N_FSDP, FSDP_ROWS)

    def step(carry, item):
        x_part, dy_part, dom_part = item
        onehot = (dom_part[:, None] == jnp.arange(DOMAIN_COUNT, dtype=jnp.int32)[None, :]).astype(jnp.int32)
        before = jnp.cumsum(onehot, axis=0) - onehot
        position = jnp.sum(before * onehot, axis=1).astype(jnp.int32)
        place = (dom_part * slot_count + position).astype(jnp.int32)
        x_buf = jnp.zeros((DOMAIN_COUNT * slot_count, MODEL_WIDTH), jnp.float32).at[place].set(x_part.astype(jnp.float32))
        x_buf = x_buf.reshape(DOMAIN_COUNT, slot_count, MODEL_WIDTH)
        output_gradient_buffer = jnp.zeros((DOMAIN_COUNT * slot_count, VALUE_WIDTH), jnp.float32).at[place].set(dy_part.astype(jnp.float32))
        output_gradient_buffer = output_gradient_buffer.reshape(DOMAIN_COUNT, slot_count, VALUE_WIDTH)
        hidden_state = jnp.einsum('dsx,drx->dsr', x_buf, down_weight_full).astype(jnp.bfloat16)
        hidden_state = lax.optimization_barrier(hidden_state).astype(jnp.float32)
        input_gradient = (adapter_scale * jnp.einsum('cmn,cln->cml', output_gradient_buffer, up_weight_full)).astype(jnp.bfloat16)
        input_gradient = lax.optimization_barrier(input_gradient).astype(jnp.float32)
        adapter_update = (adapter_scale * jnp.einsum('txl,tlz->txz', hidden_state, up_weight_full)).astype(jnp.bfloat16)
        part_a = jnp.einsum('dsr,dsx->drx', input_gradient, x_buf)
        up_weight_partial = adapter_scale * jnp.einsum('noi,noh->nih', hidden_state, output_gradient_buffer)
        base = jnp.dot(x_part, value_weight_frozen, preferred_element_type=jnp.float32)
        adapted = adapter_update.reshape(DOMAIN_COUNT * slot_count, VALUE_WIDTH)[place].astype(jnp.float32)
        output = (base + adapted).astype(jnp.bfloat16)
        return (carry[0] + part_a, carry[1] + up_weight_partial), output

    start = (jnp.zeros((DOMAIN_COUNT, ADAPTER_RANK, MODEL_WIDTH), jnp.float32), jnp.zeros((DOMAIN_COUNT, ADAPTER_RANK, VALUE_WIDTH), jnp.float32))
    (grad_a, grad_b), outputs = lax.scan(step, start, (x_blocks, dy_blocks, dom_blocks))
    return outputs.reshape(TOKENS, VALUE_WIDTH), grad_a, grad_b
```

```python
import functools

import jax
import jax.numpy as jnp
from jax import lax
from jax.experimental import pallas as pl
from jax.experimental.pallas import tpu as pltpu
from jax.sharding import PartitionSpec as P

CAPD = 12
adapter_scale = 0.5
MESH = pl.DeviceIdType.MESH
F32 = jnp.float32
BF16 = jnp.bfloat16


def remote(src, dst, send_sem, recv_sem, device):
    return pltpu.make_async_remote_copy(
        src_ref=src, dst_ref=dst, send_sem=send_sem, recv_sem=recv_sem,
        device_id=device, device_id_type=MESH,
    )


def dot(a, b):
    return jnp.dot(a, b, preferred_element_type=F32)


def dot_nt(a, b):
    return lax.dot_general(a, b, (((1,), (1,)), ((), ())), preferred_element_type=F32)


def kernel(
    geo,
    dom_row_ref, dom_col_ref, x_hbm, w_hbm, down_hbm, up_hbm, dy_hbm,
    y_ref, ga_ref, gb_ref,
    xv, wg, av, bv, dyv,
    sdy, got_dy, sx, got_x,
    part_x, part_q, sum_v, zs, zr, full_v,
    bt, sa, sb, ra, rb, s2, r2, sgb, rgb,
    sret, ret,
    ld_sem, xs_sem, xr_sem, ds_sem, dr_sem, rs_sem, rr_sem, ws_sem, wr_sem,
    ps_sem, pr_sem, zs_sem, zr_sem, gs_sem, gr_sem, fs_sem, fr_sem,
    a1s_sem, a1r_sem, a2s_sem, a2r_sem, bs_sem, br_sem,
):
    NX, NY, NZH, NAD = geo
    NF = NX * NY
    NZ = NZH * NAD
    tokens = xv.shape[0]
    fw = av.shape[2]
    nd, rank = av.shape[0], av.shape[1]
    vw = bv.shape[2]
    wk = wg.shape[1]
    slots = nd * CAPD
    half = fw // 2
    rc = rank // NF

    fi = lax.axis_index("fsdp")
    ti = lax.axis_index("tp")
    ai = lax.axis_index("ad")
    yi, xi = lax.div(fi, NX), lax.rem(fi, NX)
    zh, core = lax.div(ti, 2), lax.rem(ti, 2)
    z = zh * NAD + ai
    sgn = 1 - 2 * core

    def zdev(k):
        zz = lax.rem(z + k + NZ, NZ)
        return lax.div(zz, NAD), lax.rem(zz, NAD)

    def fpeer(jy, jx):
        return lax.rem(yi + jy + NY, NY) * NX + lax.rem(xi + jx + NX, NX)

    def hpeer(j):
        return {"tp": lax.rem(zh + j + NZH, NZH) * 2 + core}

    partner = {"tp": zh * 2 + (1 - core)}

    ks = []
    for m in range(1, (NAD + 1) // 2):
        ks += [m, -m]
    if NAD > 1:
        ks.append((NAD // 2) * sgn)
    foff = [(j // NX, j % NX) for j in range(1, NF)]

    loads = [
        pltpu.make_async_copy(dy_hbm, dyv, ld_sem.at[0]),
        pltpu.make_async_copy(x_hbm, xv, ld_sem.at[1]),
        pltpu.make_async_copy(up_hbm, bv, ld_sem.at[2]),
        pltpu.make_async_copy(down_hbm, av, ld_sem.at[3]),
        pltpu.make_async_copy(w_hbm, wg.at[fi], ld_sem.at[4]),
    ]
    for c in loads:
        c.start()

    barrier = pltpu.get_barrier_semaphore()
    count = 0

    def greet(device):
        pl.semaphore_signal(barrier, inc=1, device_id=device, device_id_type=MESH)

    if NZH > 1:
        for j in (1, -1):
            greet(hpeer(j))
            count += 1
    for k in ks[:-1] + ([ks[-1], -ks[-1]] if ks else []):
        hh, aa = zdev(k)
        greet({"tp": hh * 2 + core, "ad": aa})
        count += 1
    for j in range(1, NAD):
        greet({"ad": lax.rem(ai + j, NAD)})
        count += 1
    for jy, jx in foff:
        greet({"fsdp": fpeer(jy, jx)})
        count += 1
    greet(partner)
    count += 1

    nall = nd * NAD
    dom_row = dom_row_ref[...].astype(F32)
    dom_col = dom_col_ref[...].astype(F32)
    ti0 = lax.broadcasted_iota(jnp.int32, (tokens, tokens), 0)
    ti1 = lax.broadcasted_iota(jnp.int32, (tokens, tokens), 1)
    oh_r = jnp.where(
        dom_row == lax.broadcasted_iota(jnp.int32, (nall, tokens), 0).astype(F32), 1.0, 0.0
    )
    oh_c = jnp.where(
        dom_col == lax.broadcasted_iota(jnp.int32, (tokens, nall), 1).astype(F32), 1.0, 0.0
    )
    before_r = dot(oh_r.astype(BF16), jnp.where(ti0 < ti1, 1.0, 0.0).astype(BF16))
    before_c = dot(jnp.where(ti1 < ti0, 1.0, 0.0).astype(BF16), oh_c.astype(BF16))
    place_r = dom_row * float(CAPD) + jnp.sum(before_r * oh_r, axis=0, keepdims=True)
    place_c = dom_col * float(CAPD) + jnp.sum(before_c * oh_c, axis=1, keepdims=True)

    def pick(dest):
        rows = lax.broadcasted_iota(jnp.int32, (slots, tokens), 0) + dest * slots
        return jnp.where(rows.astype(F32) == place_r, 1.0, 0.0).astype(BF16)

    loads[0].wait()
    dy_own = dyv[...]
    for j in range(NAD):
        aa = lax.rem(ai + j, NAD)
        out = dot(pick(aa), dy_own).astype(BF16)
        if j == 0:
            got_dy[ai] = out
        else:
            sdy[j] = out
    loads[1].wait()

    def packed(hh, aa):
        cols = pl.ds(pl.multiple_of((hh * 2 + core) * fw, fw), fw)
        return dot(pick(aa), xv[:, cols]).astype(BF16)

    for i, k in enumerate(ks):
        hh, aa = zdev(k)
        sx[i] = packed(hh, aa)

    pl.semaphore_wait(barrier, count)

    pending = []

    def go(copy):
        copy.start()
        pending.append(copy)

    for j in range(1, NAD):
        go(remote(sdy.at[j], got_dy.at[ai], ds_sem.at[j], dr_sem.at[j],
                  {"ad": lax.rem(ai + j, NAD)}))
    for i, k in enumerate(ks):
        hh, aa = zdev(k)
        go(remote(sx.at[i], got_x.at[ai], xs_sem.at[i], xr_sem.at[i],
                  {"tp": hh * 2 + core, "ad": aa}))
    for n, (jy, jx) in enumerate(foff):
        go(remote(w_hbm, wg.at[fi], ws_sem.at[n], wr_sem.at[n], {"fsdp": fpeer(jy, jx)}))

    got_x[ai] = packed(zh, ai)

    rowdom = lax.broadcasted_iota(jnp.int32, (NAD, slots, rank), 1)

    def own_rows(d):
        return (rowdom >= d * CAPD) & (rowdom < (d + 1) * CAPD)

    def share(which, value):
        for t in range(NAD):
            part_x[which, t % 2, t // 2] = value[t]
        go(remote(part_x.at[which, 1 - core], part_q.at[which],
                  ps_sem.at[which], pr_sem.at[which], partner))

    def wait_recv(dst, sem, device):
        remote(dst, dst, sem, sem, device).wait_recv()

    def ring_send(which, n, value, to):
        zs[which, n] = value.astype(BF16)
        go(remote(zs.at[which, n], zr.at[which, n], zs_sem.at[which, n], zr_sem.at[which, n],
                  hpeer(to)))

    def ring_open(which):
        wait_recv(part_q.at[which], pr_sem.at[which], partner)
        sum_v[which] = part_x[which, core] + part_q[which]
        if NZH > 1:
            ring_send(which, 0, sum_v[which, lax.rem(zh + 2, NZH)], sgn)
            ring_send(which, 2, sum_v[which, lax.rem(zh - sgn + NZH, NZH)], -sgn)

    def ring_mid(which):
        if NZH > 1:
            wait_recv(zr.at[which, 0], zr_sem.at[which, 0], hpeer(-sgn))
            own = sum_v[which, lax.rem(zh + sgn + NZH, NZH)]
            ring_send(which, 1, own + zr[which, 0].astype(F32), sgn)

    def chunk(j):
        return lax.rem(zh + j + NZH, NZH) * 2 + core

    def forward(which, n, j):
        at = full_v.at[which, chunk(j)]
        go(remote(at, at, fs_sem.at[which, n], fr_sem.at[which, n], partner))

    def gather_send(which, n, j, to):
        at = full_v.at[which, chunk(j)]
        go(remote(at, at, gs_sem.at[which, n], gr_sem.at[which, n], hpeer(to)))

    def ring_close(which, scale):
        total = sum_v[which, zh]
        if NZH > 1:
            wait_recv(zr.at[which, 1], zr_sem.at[which, 1], hpeer(-sgn))
            wait_recv(zr.at[which, 2], zr_sem.at[which, 2], hpeer(sgn))
            total = total + zr[which, 1].astype(F32) + zr[which, 2].astype(F32)
        full_v[which, chunk(0)] = (total * scale).astype(BF16)
        if NZH > 1:
            gather_send(which, 0, 0, sgn)
            gather_send(which, 1, 0, -sgn)
        forward(which, 0, 0)

    def gather_mid(which):
        if NZH > 1:
            wait_recv(full_v.at[which, chunk(-sgn)], gr_sem.at[which, 0], hpeer(-sgn))
            gather_send(which, 2, -sgn, sgn)
            forward(which, 1, -sgn)

    def gather_close(which):
        if NZH > 1:
            wait_recv(full_v.at[which, chunk(sgn)], gr_sem.at[which, 1], hpeer(sgn))
            forward(which, 2, sgn)
            wait_recv(full_v.at[which, chunk(2)], gr_sem.at[which, 2], hpeer(-sgn))
            forward(which, 3, 2)

    def gather_done(which):
        other = 1 - core
        for n, j in enumerate((0, sgn, -sgn, 2) if NZH > 1 else (0,)):
            at = full_v.at[which, lax.rem(zh + j + NZH, NZH) * 2 + other]
            wait_recv(at, fr_sem.at[which, n], partner)

    loads[2].wait()
    for j in range(1, NAD):
        src = lax.rem(ai - j + NAD, NAD)
        wait_recv(got_dy.at[src], dr_sem.at[j], {"ad": src})
    rows_dy = got_dy[...].reshape(NAD * slots, vw)
    acc = jnp.zeros((NAD, slots, rank), F32)
    for d in range(nd):
        acc = acc + jnp.where(
            own_rows(d), dot_nt(rows_dy, bv[d]).reshape(NAD, slots, rank), 0.0
        )
    share(0, acc)
    ring_open(0)

    loads[3].wait()
    for i, k in enumerate(ks):
        hh, aa = zdev(-k)
        wait_recv(got_x.at[aa], xr_sem.at[i], {"tp": hh * 2 + core, "ad": aa})
    rows_x = got_x[...].reshape(NAD * slots, fw)
    acc = jnp.zeros((NAD, slots, rank), F32)
    for d in range(nd):
        acc = acc + jnp.where(
            own_rows(d), dot_nt(rows_x, av[d]).reshape(NAD, slots, rank), 0.0
        )
    share(1, acc)
    ring_mid(0)
    ring_open(1)
    ring_close(0, adapter_scale)

    loads[4].wait()
    for n, (jy, jx) in enumerate(foff):
        src = fpeer(-jy, -jx)
        wait_recv(wg.at[src], wr_sem.at[n], {"fsdp": src})
    steps = 4 if NF % 4 == 0 else 1
    per = NF // steps

    gather_mid(0)
    ring_mid(1)
    gather_close(0)
    ring_close(1, 1.0)
    gather_done(0)

    lane = lax.broadcasted_iota(jnp.int32, (rank, NAD * slots), 1).astype(F32)
    lane = lane - float(slots) * jnp.floor((lane + 0.5) / float(slots))

    def lane_dom(d):
        return (lane >= float(d * CAPD)) & (lane < float((d + 1) * CAPD))

    back_t = full_v[0].reshape(NAD * slots, rank).astype(F32).T
    for d in range(nd):
        bt[d] = jnp.where(lane_dom(d), back_t, 0.0).astype(BF16)

    def part_a(h, dst, by_x):
        def one(d, _):
            res = dot(
                bt[d], got_x[:, :, h * half:(h + 1) * half].reshape(NAD * slots, half)
            ).astype(BF16).reshape(NF, rc, half)
            for f in range(NF):
                yy, xx = f // NX, f % NX
                if by_x:
                    dst[xx, yy, d] = res[f]
                else:
                    dst[yy, xx, d] = res[f]
            return 0

        lax.fori_loop(0, nd, one, 0)

    part_a(0, sa, True)
    for j in range(1, NX):
        xx = lax.rem(xi + j, NX)
        go(remote(sa.at[xx], ra.at[j], a1s_sem.at[0, j], a1r_sem.at[0, j],
                  {"fsdp": yi * NX + xx}))
    gather_mid(1)
    part_a(1, sb, False)
    for j in range(1, NY):
        yy = lax.rem(yi + j, NY)
        go(remote(sb.at[yy], rb.at[j], a1s_sem.at[1, j], a1r_sem.at[1, j],
                  {"fsdp": yy * NX + xi}))
    gather_close(1)

    base = jnp.zeros((tokens, vw), F32)
    base = lax.fori_loop(
        0, steps,
        lambda s, b: b + dot(
            xv[:, pl.ds(pl.multiple_of(s * (per * wk), per * wk), per * wk)],
            wg[pl.ds(s * per, per)].reshape(per * wk, vw)),
        base,
    )
    y_acc = base
    gather_done(1)

    hid = full_v[1].astype(F32)
    acc = jnp.zeros((NAD * slots, vw), F32)
    for d in range(nd):
        mine = jnp.where(own_rows(d), hid, 0.0).astype(BF16).reshape(NAD * slots, rank)
        acc = acc + dot(mine, bv[d])
    sret[...] = (adapter_scale * acc).astype(BF16).reshape(NAD, slots, vw)
    hid_t = hid.reshape(NAD * slots, rank).T
    rows_dy = got_dy[...].reshape(NAD * slots, vw)
    for j in range(1, NAD):
        aa = lax.rem(ai + j, NAD)
        go(remote(sret.at[aa], ret.at[ai], rs_sem.at[j], rr_sem.at[j], {"ad": aa}))
    ret[ai] = sret[ai]
    for d in range(nd):
        mine = jnp.where(lane_dom(d), hid_t, 0.0).astype(BF16)
        res = (adapter_scale * dot(mine, rows_dy)).astype(BF16).reshape(NF, rc, vw)
        for f in range(NF):
            sgb[f, d] = res[f]
    for n, (jy, jx) in enumerate(foff):
        dst = fpeer(jy, jx)
        go(remote(sgb.at[dst], rgb.at[n + 1], bs_sem.at[n], br_sem.at[n], {"fsdp": dst}))

    for j in range(1, NX):
        src = {"fsdp": yi * NX + lax.rem(xi - j + NX, NX)}
        wait_recv(ra.at[j], a1r_sem.at[0, j], src)
    for i in range(NY):
        yy = lax.rem(yi + i, NY)
        tot = sa[xi, yy].astype(F32)
        for j in range(1, NX):
            tot = tot + ra[j, yy].astype(F32)
        s2[0, i] = tot
    for i in range(1, NY):
        dst = {"fsdp": lax.rem(yi + i, NY) * NX + xi}
        go(remote(s2.at[0, i], r2.at[0, i], a2s_sem.at[0, i], a2r_sem.at[0, i], dst))
    for j in range(1, NY):
        src = {"fsdp": lax.rem(yi - j + NY, NY) * NX + xi}
        wait_recv(rb.at[j], a1r_sem.at[1, j], src)
    for i in range(NX):
        xx = lax.rem(xi + i, NX)
        tot = sb[yi, xx].astype(F32)
        for j in range(1, NY):
            tot = tot + rb[j, xx].astype(F32)
        s2[1, i] = tot
    for i in range(1, NX):
        dst = {"fsdp": yi * NX + lax.rem(xi + i, NX)}
        go(remote(s2.at[1, i], r2.at[1, i], a2s_sem.at[1, i], a2r_sem.at[1, i], dst))

    for j in range(1, NAD):
        src = lax.rem(ai - j + NAD, NAD)
        wait_recv(ret.at[src], rr_sem.at[j], {"ad": src})
    cols = lax.broadcasted_iota(jnp.int32, (tokens, NAD * slots), 1).astype(F32)
    unpick = jnp.where(cols == place_c, 1.0, 0.0).astype(BF16)
    y_acc = y_acc + dot(unpick, ret[...].reshape(NAD * slots, vw))
    y_ref[...] = y_acc.astype(BF16)

    tot = sgb[fi].astype(F32)
    for n, (jy, jx) in enumerate(foff):
        wait_recv(rgb.at[n + 1], br_sem.at[n], {"fsdp": fpeer(-jy, -jx)})
        tot = tot + rgb[n + 1].astype(F32)
    gb_ref[...] = tot
    for h, count_h in ((0, NY), (1, NX)):
        tot = s2[h, 0]
        for i in range(1, count_h):
            if h == 0:
                src = {"fsdp": lax.rem(yi - i + NY, NY) * NX + xi}
            else:
                src = {"fsdp": yi * NX + lax.rem(xi - i + NX, NX)}
            wait_recv(r2.at[h, i], a2r_sem.at[h, i], src)
            tot = tot + r2[h, i]
        ga_ref[:, :, h * half:(h + 1) * half] = tot

    for copy in pending:
        copy.wait_send()


def body(geo, x, w, down, up, dy, domain):
    NX, NY, NZH, NAD = geo
    NF = NX * NY
    tokens = x.shape[0]
    nd, rank, fw = down.shape
    vw = up.shape[2]
    slots = nd * CAPD
    half = fw // 2
    rc = rank // NF
    dom = domain[:, 0]
    V, D = pltpu.VMEM, pltpu.SemaphoreType.DMA
    nz = 4
    scratch = [
        V(x.shape, BF16), V((NF,) + w.shape, BF16), V(down.shape, BF16), V(up.shape, BF16),
        V(dy.shape, BF16),
        V((NAD, slots, vw), BF16), V((NAD, slots, vw), BF16),
        V((NAD, slots, fw), BF16), V((NAD, slots, fw), BF16),
        V((2, 2, NAD // 2, slots, rank), F32), V((2, NAD // 2, slots, rank), F32),
        V((2, NAD // 2, slots, rank), F32),
        V((2, 3, slots, rank), BF16), V((2, 3, slots, rank), BF16),
        V((2, NAD, slots, rank), BF16),
        V((nd, rank, NAD * slots), BF16),
        V((NX, NY, nd, rc, half), BF16), V((NY, NX, nd, rc, half), BF16),
        V((NX, NY, nd, rc, half), BF16), V((NY, NX, nd, rc, half), BF16),
        V((2, max(NX, NY), nd, rc, half), F32), V((2, max(NX, NY), nd, rc, half), F32),
        V((NF, nd, rc, vw), BF16), V((NF, nd, rc, vw), BF16),
        V((NAD, slots, vw), BF16), V((NAD, slots, vw), BF16),
        D((5,)), D((8,)), D((8,)), D((8,)), D((8,)), D((8,)), D((8,)), D((16,)), D((16,)),
        D((2,)), D((2,)), D((2, 3)), D((2, 3)), D((2, 3)), D((2, 3)), D((2, 4)), D((2, 4)),
        D((2, 4)), D((2, 4)), D((2, 4)), D((2, 4)), D((16,)), D((16,)),
    ]
    vm = pl.BlockSpec(memory_space=pltpu.VMEM)
    hbm = pl.BlockSpec(memory_space=pl.ANY)
    return pl.pallas_call(
        functools.partial(kernel, geo),
        out_shape=(
            jax.ShapeDtypeStruct((tokens, vw), BF16),
            jax.ShapeDtypeStruct((nd, rc, fw), F32),
            jax.ShapeDtypeStruct((nd, rc, vw), F32),
        ),
        in_specs=[vm, vm, hbm, hbm, hbm, hbm, hbm],
        out_specs=(vm, vm, vm),
        scratch_shapes=scratch,
        compiler_params=pltpu.CompilerParams(
            collective_id=0, has_side_effects=True, vmem_limit_bytes=60 * 1024 * 1024
        ),
        name="adapters",
    )(dom.reshape(1, tokens), domain, x, w, down, up, dy)


def geometry(mesh):
    side = 4 if mesh.shape["fsdp"] == 16 else 1
    return (side, mesh.shape["fsdp"] // side, mesh.shape["tp"] // 2, mesh.shape["ad"])


def solution(mesh):
    placed = (
        P(("fsdp", "ad"), None),
        P("fsdp", "tp"),
        P("ad", None, "tp"),
        P("ad", None, "tp"),
        P(("fsdp", "ad"), "tp"),
        P(("fsdp", "ad"), None),
    )
    return jax.shard_map(
        functools.partial(body, geometry(mesh)),
        mesh=mesh,
        in_specs=placed,
        out_specs=(P(("fsdp", "ad"), "tp"), P("ad", "fsdp", "tp"), P("ad", "fsdp", "tp")),
        check_vma=False,
    )
```

```python
import functools

import jax
import jax.numpy as jnp
from jax import lax
from jax.experimental import pallas as pl
from jax.experimental.pallas import tpu as pltpu
from jax.sharding import PartitionSpec as P

CAPD = 12
adapter_scale = 0.5
EARLY = 4
VLIM = 61
MESH = pl.DeviceIdType.MESH
F32 = jnp.float32
BF16 = jnp.bfloat16


def remote(src, dst, send_sem, recv_sem, device):
    return pltpu.make_async_remote_copy(
        src_ref=src, dst_ref=dst, send_sem=send_sem, recv_sem=recv_sem,
        device_id=device, device_id_type=MESH,
    )


def dot(a, b):
    return jnp.dot(a, b, preferred_element_type=F32)


def dot_nt(a, b):
    return lax.dot_general(a, b, (((1,), (1,)), ((), ())), preferred_element_type=F32)


def kernel(
    geo,
    dom_ref, x_hbm, w_hbm, down_hbm, up_hbm, dy_hbm,
    y_ref, ga_ref, gb_ref,
    xv, wg, av, bv, dyv, base_v,
    sdy, got_dy, sx, got_x,
    part_x, part_q, sum_v, zs, zr, full_v,
    bt, st, rt, s2, r2, sgb, rgb,
    sret, ret,
    ld_sem, lx_sem, xs_sem, xr_sem, ds_sem, dr_sem, rs_sem, rr_sem, ws_sem, wr_sem,
    ps_sem, pr_sem, zs_sem, zr_sem, gs_sem, gr_sem, fs_sem, fr_sem,
    a1s_sem, a1r_sem, a2s_sem, a2r_sem, bs_sem, br_sem,
):
    NX, NZH, NAD = geo
    NF = NX * NX
    NZ = NZH * NAD
    NT = 2 * NZH
    tokens = xv.shape[1]
    fw = av.shape[2]
    nd, rank = av.shape[0], av.shape[1]
    vw = bv.shape[2]
    wk = wg.shape[1]
    slots = nd * CAPD
    half = fw // 2
    rc = rank // NF

    fi = lax.axis_index("fsdp")
    ti = lax.axis_index("tp")
    ai = lax.axis_index("ad")
    yi, xi = lax.div(fi, NX), lax.rem(fi, NX)
    zh, core = lax.div(ti, 2), lax.rem(ti, 2)
    z = zh * NAD + ai
    sgn = 1 - 2 * core
    other = 1 - core

    def zdev(k):
        zz = lax.rem(z + k + NZ, NZ)
        return lax.div(zz, NAD), lax.rem(zz, NAD)

    def near(k):
        return lax.rem(ai + k + NAD, NAD)

    def fpeer(jy, jx):
        return lax.rem(yi + jy + NX, NX) * NX + lax.rem(xi + jx + NX, NX)

    def hrow(j):
        return lax.rem(zh + j + NZH, NZH)

    def hpeer(j):
        return {"tp": hrow(j) * 2 + core}

    partner = {"tp": zh * 2 + other}

    ks = [0, (NAD // 2) * sgn]
    for m in range(NAD // 2 - 1, 0, -1):
        ks += [m, -m]
    groups = NAD // 2
    foff = [(j // NX, j % NX) for j in range(1, NF)]

    load_dy = pltpu.make_async_copy(dy_hbm, dyv, ld_sem.at[0])
    load_up = pltpu.make_async_copy(up_hbm, bv, ld_sem.at[1])
    load_down = pltpu.make_async_copy(down_hbm, av, ld_sem.at[2])
    load_w = pltpu.make_async_copy(w_hbm, wg.at[fi], ld_sem.at[3])
    load_dy.start()
    load_x = []
    for n in range(NT):
        blk = hrow((0, 1, -1, 2)[n // 2]) * 2 + (core if n % 2 == 0 else other)
        load_x.append((blk, n))
    load_x = load_x[0::2] + load_x[1::2]
    load_x = [
        pltpu.make_async_copy(
            x_hbm.at[:, pl.ds(pl.multiple_of(blk * fw, fw), fw)], xv.at[blk], lx_sem.at[n])
        for blk, n in load_x
    ]
    for c in load_x[:3]:
        c.start()
    load_up.start()
    load_down.start()
    load_w.start()
    for c in load_x[3:]:
        c.start()

    barrier = pltpu.get_barrier_semaphore()
    count = 0

    def greet(device):
        pl.semaphore_signal(barrier, inc=1, device_id=device, device_id_type=MESH)

    for j in (1, -1):
        greet(hpeer(j))
        count += 1
    for k in ks[1:] + [-ks[1]]:
        hh, aa = zdev(k)
        greet({"tp": hh * 2 + core, "ad": aa})
        count += 1
    for j in range(1, NAD):
        greet({"ad": lax.rem(ai + j, NAD)})
        count += 1
    for jy, jx in foff:
        greet({"fsdp": fpeer(jy, jx)})
        count += 1
    greet(partner)
    count += 1

    nall = nd * NAD
    dom_row = dom_ref[...].astype(F32)
    ti0 = lax.broadcasted_iota(jnp.int32, (tokens, tokens), 0)
    ti1 = lax.broadcasted_iota(jnp.int32, (tokens, tokens), 1)
    oh_r = jnp.where(
        dom_row == lax.broadcasted_iota(jnp.int32, (nall, tokens), 0).astype(F32), 1.0, 0.0
    )
    before_r = dot(oh_r.astype(BF16), jnp.where(ti0 < ti1, 1.0, 0.0).astype(BF16))
    place_r = dom_row * float(CAPD) + jnp.sum(before_r * oh_r, axis=0, keepdims=True)

    def pick(dest):
        rows = lax.broadcasted_iota(jnp.int32, (slots, tokens), 0) + dest * slots
        return jnp.where(rows.astype(F32) == place_r, 1.0, 0.0).astype(BF16)

    pending = []

    def go(copy):
        copy.start()
        pending.append(copy)

    load_dy.wait()
    dy_own = dyv[...]
    for i, k in enumerate(ks):
        out = dot(pick(near(k)), dy_own).astype(BF16)
        if i == 0:
            got_dy[0] = out
        else:
            sdy[i] = out
    for c in load_x[:3]:
        c.wait()

    def packed(k):
        hh, aa = zdev(k)
        return dot(pick(aa), xv[hh * 2 + core]).astype(BF16)

    def x_send(i):
        hh, aa = zdev(ks[i])
        go(remote(sx.at[i], got_x.at[i], xs_sem.at[i], xr_sem.at[i],
                  {"tp": hh * 2 + core, "ad": aa}))

    sx[1] = packed(ks[1])
    pl.semaphore_wait(barrier, count)

    for i in range(1, NAD):
        go(remote(sdy.at[i], got_dy.at[i], ds_sem.at[i], dr_sem.at[i], {"ad": near(ks[i])}))
    x_send(1)
    for i in range(2, 4):
        sx[i] = packed(ks[i])
    for i in range(2, 4):
        x_send(i)
    for n, (jy, jx) in enumerate(foff):
        go(remote(w_hbm, wg.at[fi], ws_sem.at[n], wr_sem.at[n], {"fsdp": fpeer(jy, jx)}))
    for i in range(4, EARLY):
        sx[i] = packed(ks[i])
        x_send(i)

    rowdom = lax.broadcasted_iota(jnp.int32, (NAD, slots, rank), 1)

    def own_rows(d, n):
        return (rowdom[:n] >= d * CAPD) & (rowdom[:n] < (d + 1) * CAPD)

    def wait_recv(dst, sem, device):
        remote(dst, dst, sem, sem, device).wait_recv()

    def partial(rows, weight, n):
        acc = jnp.zeros((n, slots, rank), F32)
        for d in range(nd):
            acc = acc + jnp.where(
                own_rows(d, n), dot_nt(rows, weight[d]).reshape(n, slots, rank), 0.0
            )
        return acc

    def share(which, g, value):
        part_x[which, 0, g] = value[0]
        part_x[which, 1, g] = value[1]
        go(remote(part_x.at[which, other, g], part_q.at[which, g],
                  ps_sem.at[which, g], pr_sem.at[which, g], partner))

    def merge(which, g):
        wait_recv(part_q.at[which, g], pr_sem.at[which, g], partner)
        sum_v[which, g] = part_x[which, core, g] + part_q[which, g]

    def chunk(j):
        return hrow(j) * 2 + core

    ring = [[remote(zs.at[w, n], zr.at[w, n], zs_sem.at[w, n], zr_sem.at[w, n], hpeer(to))
             for n, to in enumerate((sgn, sgn, -sgn))] for w in range(2)]
    spread = [[remote(full_v.at[w, chunk(j)], full_v.at[w, chunk(j)], gs_sem.at[w, n],
                      gr_sem.at[w, n], hpeer(to))
               for n, (j, to) in enumerate(((0, sgn), (0, -sgn), (-sgn, sgn)))] for w in range(2)]
    across = [[remote(full_v.at[w, chunk(j)], full_v.at[w, chunk(j)], fs_sem.at[w, n],
                      fr_sem.at[w, n], partner)
               for n, j in enumerate((0, -sgn, sgn, 2))] for w in range(2)]
    for w in range(2):
        pending.extend(ring[w] + spread[w] + across[w])

    def ring_first(which):
        zs[which, 0] = sum_v[which, hrow(2)].astype(BF16)
        ring[which][0].start()

    def ring_side(which):
        zs[which, 2] = sum_v[which, hrow(-sgn)].astype(BF16)
        ring[which][2].start()

    def ring_mid(which):
        wait_recv(zr.at[which, 0], zr_sem.at[which, 0], hpeer(-sgn))
        zs[which, 1] = (sum_v[which, hrow(sgn)] + zr[which, 0].astype(F32)).astype(BF16)
        ring[which][1].start()

    def ring_close(which, scale):
        wait_recv(zr.at[which, 2], zr_sem.at[which, 2], hpeer(sgn))
        wait_recv(zr.at[which, 1], zr_sem.at[which, 1], hpeer(-sgn))
        total = sum_v[which, zh] + zr[which, 1].astype(F32) + zr[which, 2].astype(F32)
        full_v[which, chunk(0)] = (total * scale).astype(BF16)
        spread[which][0].start()
        spread[which][1].start()
        across[which][0].start()

    def gather_mid(which):
        wait_recv(full_v.at[which, chunk(-sgn)], gr_sem.at[which, 0], hpeer(-sgn))
        spread[which][2].start()
        across[which][1].start()

    def gather_side(which):
        wait_recv(full_v.at[which, chunk(sgn)], gr_sem.at[which, 1], hpeer(sgn))
        across[which][2].start()

    def gather_close(which):
        wait_recv(full_v.at[which, chunk(2)], gr_sem.at[which, 2], hpeer(-sgn))
        across[which][3].start()

    def gather_done(which):
        for n, j in enumerate((0, sgn, -sgn, 2)):
            wait_recv(full_v.at[which, hrow(j) * 2 + other], fr_sem.at[which, n], partner)

    def at_row(g, j, step):
        @pl.when(hrow(j) == g)
        def _():
            step()

    def open_row(g):
        merge(1, g)
        at_row(g, 2, lambda: ring_first(1))
        at_row(g, -sgn, lambda: ring_side(1))

    def mid_row(g):
        at_row(g, sgn, lambda: ring_mid(1))

    def close_row(g):
        at_row(g, 0, lambda: ring_close(1, 1.0))

    def spread_row(g):
        at_row(g, -sgn, lambda: gather_mid(1))
        at_row(g, sgn, lambda: gather_side(1))

    def end_row(g):
        at_row(g, 2, lambda: gather_close(1))

    load_up.wait()
    for i in range(1, NAD):
        wait_recv(got_dy.at[i], dr_sem.at[i], {"ad": near(-ks[i])})
    value = partial(got_dy[...].reshape(NAD * slots, vw), bv, NAD)
    for g in range(groups):
        share(0, g, value[2 * g:2 * g + 2])
    for i in range(max(4, EARLY), NAD):
        sx[i] = packed(ks[i])
    for g in range(groups):
        merge(0, g)
    ring_first(0)
    ring_side(0)
    for i in range(max(4, EARLY), NAD):
        x_send(i)
    got_x[0] = packed(0)

    load_down.wait()

    def hidden_group(g):
        for i in (2 * g, 2 * g + 1):
            if i > 0:
                hh, aa = zdev(-ks[i])
                wait_recv(got_x.at[i], xr_sem.at[i], {"tp": hh * 2 + core, "ad": aa})
        share(1, g, partial(got_x[2 * g:2 * g + 2].reshape(2 * slots, fw), av, 2))

    per = NF // NT

    def base_step(n, _):
        rows = wg[pl.ds(n * per, per)].reshape(per * wk, vw)
        base_v[...] = base_v[...] + dot(xv[n], rows)
        return 0

    def base():
        for c in load_x[3:]:
            c.wait()
        load_w.wait()
        for n, (jy, jx) in enumerate(foff):
            src = fpeer(-jy, -jx)
            wait_recv(wg.at[src], wr_sem.at[n], {"fsdp": src})
        base_v[...] = jnp.zeros_like(base_v)
        lax.fori_loop(0, NT, base_step, 0)

    lane = lax.broadcasted_iota(jnp.int32, (rank, NAD * slots), 1).astype(F32)
    lane = lane - float(slots) * jnp.floor((lane + 0.5) / float(slots))

    def lane_dom(d):
        return (lane >= float(d * CAPD)) & (lane < float((d + 1) * CAPD))

    def prepare_a():
        back_t = full_v[0].reshape(NAD * slots, rank).astype(F32).T
        for d in range(nd):
            bt[d] = jnp.where(lane_dom(d), back_t, 0.0).astype(BF16)

    pairs = nd // 2
    line = (xi, yi)

    def axis_peer(h, j):
        if h == 0:
            return {"fsdp": fpeer(0, j)}
        return {"fsdp": fpeer(j, 0)}

    def part_a(h, p):
        def one(e, _):
            res = dot(
                bt[p * 2 + e], got_x[:, :, h * half:(h + 1) * half].reshape(NAD * slots, half)
            ).astype(BF16).reshape(NF, rc, half)
            for f in range(NF):
                yx = (f // NX, f % NX)
                st[h, p, yx[1 - h], yx[h], e] = res[f]
            return 0

        lax.fori_loop(0, 2, one, 0)
        for j in range(1, NX):
            go(remote(st.at[h, p, lax.rem(line[h] + j, NX)], rt.at[h, p, j],
                      a1s_sem.at[h, p, j], a1r_sem.at[h, p, j], axis_peer(h, j)))

    def fold_a(h, p):
        for j in range(1, NX):
            wait_recv(rt.at[h, p, j], a1r_sem.at[h, p, j], axis_peer(h, -j))
        for i in range(NX):
            at = lax.rem(line[1 - h] + i, NX)
            tot = st[h, p, line[h], at].astype(F32)
            for j in range(1, NX):
                tot = tot + rt[h, p, j, at].astype(F32)
            s2[h, p, i] = tot
        for i in range(1, NX):
            go(remote(s2.at[h, p, i], r2.at[h, p, i], a2s_sem.at[h, p, i], a2r_sem.at[h, p, i],
                      axis_peer(1 - h, i)))

    pieces = [(h, p) for p in range(pairs) for h in range(2)]
    hidden_group(0)
    open_row(0)
    hidden_group(1)
    open_row(1)
    ring_mid(0)
    hidden_group(2)
    open_row(2)
    hidden_group(3)
    open_row(3)
    ring_close(0, adapter_scale)
    mid_row(0)
    mid_row(1)
    mid_row(2)
    mid_row(3)
    gather_mid(0)
    gather_side(0)
    base()
    close_row(0)
    close_row(1)
    close_row(2)
    close_row(3)
    gather_close(0)
    gather_done(0)
    prepare_a()
    part_a(*pieces[0])
    part_a(*pieces[1])
    spread_row(0)
    spread_row(1)
    spread_row(2)
    spread_row(3)
    part_a(*pieces[2])
    part_a(*pieces[3])
    fold_a(*pieces[0])
    fold_a(*pieces[1])
    end_row(0)
    end_row(1)
    end_row(2)
    end_row(3)
    gather_done(1)

    hid = full_v[1].astype(F32)
    acc = jnp.zeros((NAD * slots, vw), F32)
    for d in range(nd):
        mine = jnp.where(own_rows(d, NAD), hid, 0.0).astype(BF16).reshape(NAD * slots, rank)
        acc = acc + dot(mine, bv[d])
    sret[...] = (adapter_scale * acc).astype(BF16).reshape(NAD, slots, vw)
    hid_t = hid.reshape(NAD * slots, rank).T
    for i in range(1, NAD):
        go(remote(sret.at[i], ret.at[i], rs_sem.at[i], rr_sem.at[i], {"ad": near(-ks[i])}))
    ret[0] = sret[0]
    rows_dy = got_dy[...].reshape(NAD * slots, vw)
    for d in range(nd):
        mine = jnp.where(lane_dom(d), hid_t, 0.0).astype(BF16)
        res = (adapter_scale * dot(mine, rows_dy)).astype(BF16).reshape(NF, rc, vw)
        for f in range(NF):
            sgb[f, d] = res[f]
    for n, (jy, jx) in enumerate(foff):
        dst = fpeer(jy, jx)
        go(remote(sgb.at[dst], rgb.at[n + 1], bs_sem.at[n], br_sem.at[n], {"fsdp": dst}))
    fold_a(*pieces[2])
    fold_a(*pieces[3])

    place_c = jnp.broadcast_to(place_r, (128, tokens)).T[:, 0:1]
    col = lax.broadcasted_iota(jnp.int32, (1, NAD * slots), 1)
    ident = jnp.zeros((1, NAD * slots), jnp.int32)
    for i, k in enumerate(ks):
        inside = (col >= i * slots) & (col < (i + 1) * slots)
        ident = jnp.where(inside, col + (near(k) - i) * slots, ident)
    unpick = jnp.where(ident.astype(F32) == place_c, 1.0, 0.0).astype(BF16)
    for i in range(1, NAD):
        wait_recv(ret.at[i], rr_sem.at[i], {"ad": near(ks[i])})
    y_ref[...] = (base_v[...] + dot(unpick, ret[...].reshape(NAD * slots, vw))).astype(BF16)

    tot = sgb[fi].astype(F32)
    for n, (jy, jx) in enumerate(foff):
        wait_recv(rgb.at[n + 1], br_sem.at[n], {"fsdp": fpeer(-jy, -jx)})
        tot = tot + rgb[n + 1].astype(F32)
    gb_ref[...] = tot
    for h, p in pieces:
        tot = s2[h, p, 0]
        for i in range(1, NX):
            wait_recv(r2.at[h, p, i], a2r_sem.at[h, p, i], axis_peer(1 - h, -i))
            tot = tot + r2[h, p, i]
        ga_ref[2 * p:2 * p + 2, :, h * half:(h + 1) * half] = tot

    for copy in pending:
        copy.wait_send()


def finish(y_in, ga_in, gb_in, y_ref, ga_ref, gb_ref):
    y_ref[...] = y_in[...]
    ga_ref[...] = ga_in[...]
    gb_ref[...] = gb_in[...]


def body(geo, x, w, down, up, dy, domain):
    NX, NZH, NAD = geo
    NF = NX * NX
    NT = 2 * NZH
    tokens = x.shape[0]
    nd, rank, fw = down.shape
    vw = up.shape[2]
    slots = nd * CAPD
    half = fw // 2
    rc = rank // NF
    pairs = nd // 2
    V, D = pltpu.VMEM, pltpu.SemaphoreType.DMA
    scratch = [
        V((NT, tokens, fw), BF16), V((NF,) + w.shape, BF16), V(down.shape, BF16),
        V(up.shape, BF16), V(dy.shape, BF16), V((tokens, vw), F32),
        V((NAD, slots, vw), BF16), V((NAD, slots, vw), BF16),
        V((NAD, slots, fw), BF16), V((NAD, slots, fw), BF16),
        V((2, 2, NZH, slots, rank), F32), V((2, NZH, slots, rank), F32),
        V((2, NZH, slots, rank), F32),
        V((2, 3, slots, rank), BF16), V((2, 3, slots, rank), BF16),
        V((2, NAD, slots, rank), BF16),
        V((nd, rank, NAD * slots), BF16),
        V((2, pairs, NX, NX, 2, rc, half), BF16), V((2, pairs, NX, NX, 2, rc, half), BF16),
        V((2, pairs, NX, 2, rc, half), F32), V((2, pairs, NX, 2, rc, half), F32),
        V((NF, nd, rc, vw), BF16), V((NF, nd, rc, vw), BF16),
        V((NAD, slots, vw), BF16), V((NAD, slots, vw), BF16),
        D((4,)), D((NT,)),
        D((NAD,)), D((NAD,)), D((NAD,)), D((NAD,)), D((NAD,)), D((NAD,)), D((NF,)), D((NF,)),
        D((2, NZH)), D((2, NZH)), D((2, 3)), D((2, 3)), D((2, 3)), D((2, 3)), D((2, 4)), D((2, 4)),
        D((2, pairs, NX)), D((2, pairs, NX)), D((2, pairs, NX)), D((2, pairs, NX)),
        D((NF,)), D((NF,)),
    ]
    vm = pl.BlockSpec(memory_space=pltpu.VMEM)
    hbm = pl.BlockSpec(memory_space=pltpu.HBM)
    shapes = (
        jax.ShapeDtypeStruct((tokens, vw), BF16),
        jax.ShapeDtypeStruct((nd, rc, fw), F32),
        jax.ShapeDtypeStruct((nd, rc, vw), F32),
    )
    results = pl.pallas_call(
        functools.partial(kernel, geo),
        out_shape=shapes,
        in_specs=[vm, hbm, hbm, hbm, hbm, hbm],
        out_specs=(vm, vm, vm),
        scratch_shapes=scratch,
        compiler_params=pltpu.CompilerParams(
            collective_id=0, has_side_effects=True, vmem_limit_bytes=VLIM * 1024 * 1024
        ),
        name="adapters",
    )(domain.reshape(1, tokens), x, w, down, up, dy)
    return tuple(
        pl.pallas_call(
            finish, out_shape=shapes, in_specs=[vm, vm, vm], out_specs=(vm, vm, vm),
            compiler_params=pltpu.CompilerParams(vmem_limit_bytes=8 * 1024 * 1024),
            name="finish",
        )(*results)
    )


def geometry(mesh):
    return (4, mesh.shape["tp"] // 2, mesh.shape["ad"])


def solution(mesh):
    placed = (
        P(("fsdp", "ad"), None),
        P("fsdp", "tp"),
        P("ad", None, "tp"),
        P("ad", None, "tp"),
        P(("fsdp", "ad"), "tp"),
        P(("fsdp", "ad"), None),
    )
    return jax.shard_map(
        functools.partial(body, geometry(mesh)),
        mesh=mesh,
        in_specs=placed,
        out_specs=(P(("fsdp", "ad"), "tp"), P("ad", "fsdp", "tp"), P("ad", "fsdp", "tp")),
        check_vma=False,
    )
```

```python
import functools

import jax
import jax.numpy as jnp
from jax import lax
from jax.experimental import pallas as pl
from jax.experimental.pallas import tpu as pltpu
from jax.sharding import PartitionSpec as P

CAPD = 12
adapter_scale = 0.5
EARLY = 4
VLIM = 63
MESH = pl.DeviceIdType.MESH
F32 = jnp.float32
BF16 = jnp.bfloat16


def remote(src, dst, send_sem, recv_sem, device):
    return pltpu.make_async_remote_copy(
        src_ref=src, dst_ref=dst, send_sem=send_sem, recv_sem=recv_sem,
        device_id=device, device_id_type=MESH,
    )


def dot(a, b):
    return jnp.dot(a, b, preferred_element_type=F32)


def dot_nt(a, b):
    return lax.dot_general(a, b, (((1,), (1,)), ((), ())), preferred_element_type=F32)


def kernel(
    geo,
    dom_ref, x_hbm, w_hbm, down_hbm, up_hbm, dy_hbm,
    y_ref, ga_ref, gb_ref,
    xv, wg, av, bv, dyv, base_v,
    sdy, got_dy, sx, got_x,
    part_x, part_q, sum_v, zs, zr, full_v,
    bt, st, rt, s2, r2, sgb, rgb,
    sret, ret,
    ld_sem, lx_sem, xs_sem, xr_sem, ds_sem, dr_sem, rs_sem, rr_sem, ws_sem, wr_sem,
    ps_sem, pr_sem, zs_sem, zr_sem, gs_sem, gr_sem, fs_sem, fr_sem,
    a1s_sem, a1r_sem, a2s_sem, a2r_sem, bs_sem, br_sem,
):
    NX, NZH, NAD = geo
    NF = NX * NX
    NZ = NZH * NAD
    NT = 2 * NZH
    tokens = xv.shape[1]
    fw = av.shape[2]
    nd, rank = av.shape[0], av.shape[1]
    vw = bv.shape[2]
    wk = wg.shape[1]
    slots = nd * CAPD
    half = fw // 2
    rc = rank // NF

    fi = lax.axis_index("fsdp")
    ti = lax.axis_index("tp")
    ai = lax.axis_index("ad")
    yi, xi = lax.div(fi, NX), lax.rem(fi, NX)
    zh, core = lax.div(ti, 2), lax.rem(ti, 2)
    z = zh * NAD + ai
    sgn = 1 - 2 * core
    other = 1 - core

    def zdev(k):
        zz = lax.rem(z + k + NZ, NZ)
        return lax.div(zz, NAD), lax.rem(zz, NAD)

    def near(k):
        return lax.rem(ai + k + NAD, NAD)

    def fpeer(jy, jx):
        return lax.rem(yi + jy + NX, NX) * NX + lax.rem(xi + jx + NX, NX)

    def hrow(j):
        return lax.rem(zh + j + NZH, NZH)

    def hpeer(j):
        return {"tp": hrow(j) * 2 + core}

    partner = {"tp": zh * 2 + other}

    ks = [0, (NAD // 2) * sgn]
    for m in range(NAD // 2 - 1, 0, -1):
        ks += [m, -m]
    groups = NAD // 2
    foff = [(j // NX, j % NX) for j in range(1, NF)]

    load_dy = pltpu.make_async_copy(dy_hbm, dyv, ld_sem.at[0])
    load_up = pltpu.make_async_copy(up_hbm, bv, ld_sem.at[1])
    load_down = pltpu.make_async_copy(down_hbm, av, ld_sem.at[2])
    load_w = pltpu.make_async_copy(w_hbm, wg.at[fi], ld_sem.at[3])
    load_dy.start()
    load_x = []
    for n in range(NT):
        blk = hrow((0, 1, -1, 2)[n // 2]) * 2 + (core if n % 2 == 0 else other)
        load_x.append((blk, n))
    load_x = load_x[0::2] + load_x[1::2]
    load_x = [
        pltpu.make_async_copy(
            x_hbm.at[:, pl.ds(pl.multiple_of(blk * fw, fw), fw)], xv.at[blk], lx_sem.at[n])
        for blk, n in load_x
    ]
    for c in load_x[:3]:
        c.start()
    load_up.start()
    load_down.start()
    load_w.start()
    for c in load_x[3:]:
        c.start()

    barrier = pltpu.get_barrier_semaphore()
    count = 0

    def greet(device):
        pl.semaphore_signal(barrier, inc=1, device_id=device, device_id_type=MESH)

    for j in (1, -1):
        greet(hpeer(j))
        count += 1
    for k in ks[1:] + [-ks[1]]:
        hh, aa = zdev(k)
        greet({"tp": hh * 2 + core, "ad": aa})
        count += 1
    for j in range(1, NAD):
        greet({"ad": lax.rem(ai + j, NAD)})
        count += 1
    for jy, jx in foff:
        greet({"fsdp": fpeer(jy, jx)})
        count += 1
    greet(partner)
    count += 1

    nall = nd * NAD
    dom_row = dom_ref[...].astype(F32)
    ti0 = lax.broadcasted_iota(jnp.int32, (tokens, tokens), 0)
    ti1 = lax.broadcasted_iota(jnp.int32, (tokens, tokens), 1)
    oh_r = jnp.where(
        dom_row == lax.broadcasted_iota(jnp.int32, (nall, tokens), 0).astype(F32), 1.0, 0.0
    )
    before_r = dot(oh_r.astype(BF16), jnp.where(ti0 < ti1, 1.0, 0.0).astype(BF16))
    place_r = dom_row * float(CAPD) + jnp.sum(before_r * oh_r, axis=0, keepdims=True)

    def pick(dest):
        rows = lax.broadcasted_iota(jnp.int32, (slots, tokens), 0) + dest * slots
        return jnp.where(rows.astype(F32) == place_r, 1.0, 0.0).astype(BF16)

    pending = []

    def go(copy):
        copy.start()
        pending.append(copy)

    load_dy.wait()
    dy_own = dyv[...]
    for i, k in enumerate(ks):
        out = dot(pick(near(k)), dy_own).astype(BF16)
        if i == 0:
            got_dy[0] = out
        else:
            sdy[i] = out
    for c in load_x[:3]:
        c.wait()

    def packed(k):
        hh, aa = zdev(k)
        return dot(pick(aa), xv[hh * 2 + core]).astype(BF16)

    def x_send(i):
        hh, aa = zdev(ks[i])
        go(remote(sx.at[i], got_x.at[i], xs_sem.at[i], xr_sem.at[i],
                  {"tp": hh * 2 + core, "ad": aa}))

    sx[1] = packed(ks[1])
    pl.semaphore_wait(barrier, count)

    for i in range(1, NAD):
        go(remote(sdy.at[i], got_dy.at[i], ds_sem.at[i], dr_sem.at[i], {"ad": near(ks[i])}))
    x_send(1)
    for i in range(2, 4):
        sx[i] = packed(ks[i])
    for i in range(2, 4):
        x_send(i)
    for n, (jy, jx) in enumerate(foff):
        go(remote(w_hbm, wg.at[fi], ws_sem.at[n], wr_sem.at[n], {"fsdp": fpeer(jy, jx)}))
    for i in range(4, EARLY):
        sx[i] = packed(ks[i])
        x_send(i)

    rowdom = lax.broadcasted_iota(jnp.int32, (NAD, slots, rank), 1)

    def own_rows(d, n):
        return (rowdom[:n] >= d * CAPD) & (rowdom[:n] < (d + 1) * CAPD)

    def wait_recv(dst, sem, device):
        remote(dst, dst, sem, sem, device).wait_recv()

    def partial(rows, weight, n):
        acc = jnp.zeros((n, slots, rank), F32)
        for d in range(nd):
            acc = acc + jnp.where(
                own_rows(d, n), dot_nt(rows, weight[d]).reshape(n, slots, rank), 0.0
            )
        return acc

    def share(which, g, value):
        part_x[which, 0, g] = value[0]
        part_x[which, 1, g] = value[1]
        go(remote(part_x.at[which, other, g], part_q.at[which, g],
                  ps_sem.at[which, g], pr_sem.at[which, g], partner))

    def merge(which, g):
        wait_recv(part_q.at[which, g], pr_sem.at[which, g], partner)
        sum_v[which, g] = part_x[which, core, g] + part_q[which, g]

    def chunk(j):
        return hrow(j) * 2 + core

    ring = [[remote(zs.at[w, n], zr.at[w, n], zs_sem.at[w, n], zr_sem.at[w, n], hpeer(to))
             for n, to in enumerate((sgn, sgn, -sgn))] for w in range(2)]
    spread = [[remote(full_v.at[w, chunk(j)], full_v.at[w, chunk(j)], gs_sem.at[w, n],
                      gr_sem.at[w, n], hpeer(to))
               for n, (j, to) in enumerate(((0, sgn), (0, -sgn), (-sgn, sgn)))] for w in range(2)]
    across = [[remote(full_v.at[w, chunk(j)], full_v.at[w, chunk(j)], fs_sem.at[w, n],
                      fr_sem.at[w, n], partner)
               for n, j in enumerate((0, -sgn, sgn, 2))] for w in range(2)]
    for w in range(2):
        pending.extend(ring[w] + spread[w] + across[w])

    def ring_first(which):
        zs[which, 0] = sum_v[which, hrow(2)].astype(BF16)
        ring[which][0].start()

    def ring_side(which):
        zs[which, 2] = sum_v[which, hrow(-sgn)].astype(BF16)
        ring[which][2].start()

    def ring_mid(which):
        wait_recv(zr.at[which, 0], zr_sem.at[which, 0], hpeer(-sgn))
        zs[which, 1] = (sum_v[which, hrow(sgn)] + zr[which, 0].astype(F32)).astype(BF16)
        ring[which][1].start()

    def ring_close(which, scale):
        wait_recv(zr.at[which, 2], zr_sem.at[which, 2], hpeer(sgn))
        wait_recv(zr.at[which, 1], zr_sem.at[which, 1], hpeer(-sgn))
        total = sum_v[which, zh] + zr[which, 1].astype(F32) + zr[which, 2].astype(F32)
        full_v[which, chunk(0)] = (total * scale).astype(BF16)
        spread[which][0].start()
        spread[which][1].start()
        across[which][0].start()

    def gather_mid(which):
        wait_recv(full_v.at[which, chunk(-sgn)], gr_sem.at[which, 0], hpeer(-sgn))
        spread[which][2].start()
        across[which][1].start()

    def gather_side(which):
        wait_recv(full_v.at[which, chunk(sgn)], gr_sem.at[which, 1], hpeer(sgn))
        across[which][2].start()

    def gather_close(which):
        wait_recv(full_v.at[which, chunk(2)], gr_sem.at[which, 2], hpeer(-sgn))
        across[which][3].start()

    def gather_done(which):
        for n, j in enumerate((0, sgn, -sgn, 2)):
            wait_recv(full_v.at[which, hrow(j) * 2 + other], fr_sem.at[which, n], partner)

    def at_row(g, j, step):
        @pl.when(hrow(j) == g)
        def _():
            step()

    def open_row(g):
        merge(1, g)
        at_row(g, 2, lambda: ring_first(1))
        at_row(g, -sgn, lambda: ring_side(1))

    def mid_row(g):
        at_row(g, sgn, lambda: ring_mid(1))

    def close_row(g):
        at_row(g, 0, lambda: ring_close(1, 1.0))

    def spread_row(g):
        at_row(g, -sgn, lambda: gather_mid(1))
        at_row(g, sgn, lambda: gather_side(1))

    def end_row(g):
        at_row(g, 2, lambda: gather_close(1))

    load_up.wait()
    for i in range(1, NAD):
        wait_recv(got_dy.at[i], dr_sem.at[i], {"ad": near(-ks[i])})
    value = partial(got_dy[...].reshape(NAD * slots, vw), bv, NAD)
    for g in range(groups):
        share(0, g, value[2 * g:2 * g + 2])
    for i in range(max(4, EARLY), NAD):
        sx[i] = packed(ks[i])
    for g in range(groups):
        merge(0, g)
    ring_first(0)
    ring_side(0)
    for i in range(max(4, EARLY), NAD):
        x_send(i)
    got_x[0] = packed(0)

    load_down.wait()

    def hidden_group(g):
        for i in (2 * g, 2 * g + 1):
            if i > 0:
                hh, aa = zdev(-ks[i])
                wait_recv(got_x.at[i], xr_sem.at[i], {"tp": hh * 2 + core, "ad": aa})
        share(1, g, partial(got_x[2 * g:2 * g + 2].reshape(2 * slots, fw), av, 2))

    per = NF // NT

    def base_step(n, _):
        rows = wg[pl.ds(n * per, per)].reshape(per * wk, vw)
        base_v[...] = base_v[...] + dot(xv[n], rows)
        return 0

    def base():
        for c in load_x[3:]:
            c.wait()
        load_w.wait()
        for n, (jy, jx) in enumerate(foff):
            src = fpeer(-jy, -jx)
            wait_recv(wg.at[src], wr_sem.at[n], {"fsdp": src})
        base_v[...] = jnp.zeros_like(base_v)
        lax.fori_loop(0, NT, base_step, 0)

    lane = lax.broadcasted_iota(jnp.int32, (rank, NAD * slots), 1).astype(F32)
    lane = lane - float(slots) * jnp.floor((lane + 0.5) / float(slots))

    def lane_dom(d):
        return (lane >= float(d * CAPD)) & (lane < float((d + 1) * CAPD))

    def prepare_a():
        back_t = full_v[0].reshape(NAD * slots, rank).astype(F32).T
        for d in range(nd):
            bt[d] = jnp.where(lane_dom(d), back_t, 0.0).astype(BF16)

    pairs = nd // 2
    line = (xi, yi)

    def axis_peer(h, j):
        if h == 0:
            return {"fsdp": fpeer(0, j)}
        return {"fsdp": fpeer(j, 0)}

    def part_a(h, p):
        def one(e, _):
            res = dot(
                bt[p * 2 + e], got_x[:, :, h * half:(h + 1) * half].reshape(NAD * slots, half)
            ).astype(BF16).reshape(NF, rc, half)
            for f in range(NF):
                yx = (f // NX, f % NX)
                st[h, p, yx[1 - h], yx[h], e] = res[f]
            return 0

        lax.fori_loop(0, 2, one, 0)
        for j in range(1, NX):
            go(remote(st.at[h, p, lax.rem(line[h] + j, NX)], rt.at[h, p, j],
                      a1s_sem.at[h, p, j], a1r_sem.at[h, p, j], axis_peer(h, j)))

    def fold_a(h, p):
        for j in range(1, NX):
            wait_recv(rt.at[h, p, j], a1r_sem.at[h, p, j], axis_peer(h, -j))
        for i in range(NX):
            at = lax.rem(line[1 - h] + i, NX)
            tot = st[h, p, line[h], at].astype(F32)
            for j in range(1, NX):
                tot = tot + rt[h, p, j, at].astype(F32)
            s2[h, p, i] = tot
        for i in range(1, NX):
            go(remote(s2.at[h, p, i], r2.at[h, p, i], a2s_sem.at[h, p, i], a2r_sem.at[h, p, i],
                      axis_peer(1 - h, i)))

    pieces = [(h, p) for p in range(pairs) for h in range(2)]
    hidden_group(0)
    open_row(0)
    hidden_group(1)
    open_row(1)
    ring_mid(0)
    hidden_group(2)
    open_row(2)
    hidden_group(3)
    open_row(3)
    ring_close(0, adapter_scale)
    mid_row(0)
    mid_row(1)
    mid_row(2)
    mid_row(3)
    gather_mid(0)
    gather_side(0)
    base()
    close_row(0)
    close_row(1)
    close_row(2)
    close_row(3)
    gather_close(0)
    gather_done(0)
    prepare_a()
    part_a(*pieces[0])
    part_a(*pieces[1])
    spread_row(0)
    spread_row(1)
    spread_row(2)
    spread_row(3)
    part_a(*pieces[2])
    part_a(*pieces[3])
    fold_a(*pieces[0])
    fold_a(*pieces[1])
    end_row(0)
    end_row(1)
    end_row(2)
    end_row(3)
    gather_done(1)

    hid = full_v[1].astype(F32)
    acc = jnp.zeros((NAD * slots, vw), F32)
    for d in range(nd):
        mine = jnp.where(own_rows(d, NAD), hid, 0.0).astype(BF16).reshape(NAD * slots, rank)
        acc = acc + dot(mine, bv[d])
    sret[...] = (adapter_scale * acc).astype(BF16).reshape(NAD, slots, vw)
    hid_t = hid.reshape(NAD * slots, rank).T
    for i in range(1, NAD):
        go(remote(sret.at[i], ret.at[i], rs_sem.at[i], rr_sem.at[i], {"ad": near(-ks[i])}))
    ret[0] = sret[0]
    rows_dy = got_dy[...].reshape(NAD * slots, vw)
    for d in range(nd):
        mine = jnp.where(lane_dom(d), hid_t, 0.0).astype(BF16)
        res = (adapter_scale * dot(mine, rows_dy)).astype(BF16).reshape(NF, rc, vw)
        for f in range(NF):
            sgb[f, d] = res[f]
    for n, (jy, jx) in enumerate(foff):
        dst = fpeer(jy, jx)
        go(remote(sgb.at[dst], rgb.at[n + 1], bs_sem.at[n], br_sem.at[n], {"fsdp": dst}))
    fold_a(*pieces[2])
    fold_a(*pieces[3])

    place_c = jnp.broadcast_to(place_r, (128, tokens)).T[:, 0:1]
    col = lax.broadcasted_iota(jnp.int32, (1, NAD * slots), 1)
    ident = jnp.zeros((1, NAD * slots), jnp.int32)
    for i, k in enumerate(ks):
        inside = (col >= i * slots) & (col < (i + 1) * slots)
        ident = jnp.where(inside, col + (near(k) - i) * slots, ident)
    unpick = jnp.where(ident.astype(F32) == place_c, 1.0, 0.0).astype(BF16)
    for i in range(1, NAD):
        wait_recv(ret.at[i], rr_sem.at[i], {"ad": near(ks[i])})
    y_ref[...] = (base_v[...] + dot(unpick, ret[...].reshape(NAD * slots, vw))).astype(BF16)

    tot = sgb[fi].astype(F32)
    for n, (jy, jx) in enumerate(foff):
        wait_recv(rgb.at[n + 1], br_sem.at[n], {"fsdp": fpeer(-jy, -jx)})
        tot = tot + rgb[n + 1].astype(F32)
    gb_ref[...] = tot
    for h, p in pieces:
        tot = s2[h, p, 0]
        for i in range(1, NX):
            wait_recv(r2.at[h, p, i], a2r_sem.at[h, p, i], axis_peer(1 - h, -i))
            tot = tot + r2[h, p, i]
        ga_ref[2 * p:2 * p + 2, :, h * half:(h + 1) * half] = tot

    for copy in pending:
        copy.wait_send()


def finish(y_in, ga_in, gb_in, y_ref, ga_ref, gb_ref, yv, gav, gbv, in_sem, out_sem):
    stages = ((y_in, yv, y_ref), (ga_in, gav, ga_ref), (gb_in, gbv, gb_ref))
    into = [pltpu.make_async_copy(a, v, in_sem.at[n]) for n, (a, v, _) in enumerate(stages)]
    out = [pltpu.make_async_copy(v, o, out_sem.at[n]) for n, (_, v, o) in enumerate(stages)]
    for c in into:
        c.start()
    for c, o in zip(into, out):
        c.wait()
        o.start()
    for o in out:
        o.wait()


def body(geo, x, w, down, up, dy, domain):
    NX, NZH, NAD = geo
    NF = NX * NX
    NT = 2 * NZH
    tokens = x.shape[0]
    nd, rank, fw = down.shape
    vw = up.shape[2]
    slots = nd * CAPD
    half = fw // 2
    rc = rank // NF
    pairs = nd // 2
    V, D = pltpu.VMEM, pltpu.SemaphoreType.DMA
    scratch = [
        V((NT, tokens, fw), BF16), V((NF,) + w.shape, BF16), V(down.shape, BF16),
        V(up.shape, BF16), V(dy.shape, BF16), V((tokens, vw), F32),
        V((NAD, slots, vw), BF16), V((NAD, slots, vw), BF16),
        V((NAD, slots, fw), BF16), V((NAD, slots, fw), BF16),
        V((2, 2, NZH, slots, rank), F32), V((2, NZH, slots, rank), F32),
        V((2, NZH, slots, rank), F32),
        V((2, 3, slots, rank), BF16), V((2, 3, slots, rank), BF16),
        V((2, NAD, slots, rank), BF16),
        V((nd, rank, NAD * slots), BF16),
        V((2, pairs, NX, NX, 2, rc, half), BF16), V((2, pairs, NX, NX, 2, rc, half), BF16),
        V((2, pairs, NX, 2, rc, half), F32), V((2, pairs, NX, 2, rc, half), F32),
        V((NF, nd, rc, vw), BF16), V((NF, nd, rc, vw), BF16),
        V((NAD, slots, vw), BF16), V((NAD, slots, vw), BF16),
        D((4,)), D((NT,)),
        D((NAD,)), D((NAD,)), D((NAD,)), D((NAD,)), D((NAD,)), D((NAD,)), D((NF,)), D((NF,)),
        D((2, NZH)), D((2, NZH)), D((2, 3)), D((2, 3)), D((2, 3)), D((2, 3)), D((2, 4)), D((2, 4)),
        D((2, pairs, NX)), D((2, pairs, NX)), D((2, pairs, NX)), D((2, pairs, NX)),
        D((NF,)), D((NF,)),
    ]
    vm = pl.BlockSpec(memory_space=pltpu.VMEM)
    hbm = pl.BlockSpec(memory_space=pltpu.HBM)
    shapes = (
        jax.ShapeDtypeStruct((tokens, vw), BF16),
        jax.ShapeDtypeStruct((nd, rc, fw), F32),
        jax.ShapeDtypeStruct((nd, rc, vw), F32),
    )
    results = pl.pallas_call(
        functools.partial(kernel, geo),
        out_shape=shapes,
        in_specs=[vm, hbm, hbm, hbm, hbm, hbm],
        out_specs=(vm, vm, vm),
        scratch_shapes=scratch,
        compiler_params=pltpu.CompilerParams(
            collective_id=0, has_side_effects=True, vmem_limit_bytes=VLIM * 1024 * 1024
        ),
        name="adapters",
    )(domain.reshape(1, tokens), x, w, down, up, dy)
    return tuple(
        pl.pallas_call(
            finish, out_shape=shapes, in_specs=[hbm] * 3, out_specs=(hbm,) * 3,
            scratch_shapes=[V(t.shape, t.dtype) for t in shapes] + [D((3,)), D((3,))],
            compiler_params=pltpu.CompilerParams(vmem_limit_bytes=VLIM * 1024 * 1024),
            name="finish",
        )(*results)
    )


def geometry(mesh):
    return (4, mesh.shape["tp"] // 2, mesh.shape["ad"])


def solution(mesh):
    placed = (
        P(("fsdp", "ad"), None),
        P("fsdp", "tp"),
        P("ad", None, "tp"),
        P("ad", None, "tp"),
        P(("fsdp", "ad"), "tp"),
        P(("fsdp", "ad"), None),
    )
    return jax.shard_map(
        functools.partial(body, geometry(mesh)),
        mesh=mesh,
        in_specs=placed,
        out_specs=(P(("fsdp", "ad"), "tp"), P("ad", "fsdp", "tp"), P("ad", "fsdp", "tp")),
        check_vma=False,
    )
```

```python
import functools

import jax
import jax.numpy as jnp
from jax import lax
from jax.experimental import pallas as pl
from jax.experimental.pallas import tpu as pltpu
from jax.sharding import PartitionSpec as P

CAPD = 12
adapter_scale = 0.5
EARLY = 4
VLIM = 63
MESH = pl.DeviceIdType.MESH
F32 = jnp.float32
BF16 = jnp.bfloat16


def remote(src, dst, send_sem, recv_sem, device):
    return pltpu.make_async_remote_copy(
        src_ref=src, dst_ref=dst, send_sem=send_sem, recv_sem=recv_sem,
        device_id=device, device_id_type=MESH,
    )


def dot(a, b):
    return jnp.dot(a, b, preferred_element_type=F32)


def dot_nt(a, b):
    return lax.dot_general(a, b, (((1,), (1,)), ((), ())), preferred_element_type=F32)


def kernel(
    geo,
    dom_ref, x_hbm, w_hbm, down_hbm, up_hbm, dy_hbm,
    y_ref, ga_ref, gb_ref,
    xv, wg, av, bv, dyv, base_v,
    sdy, got_dy, sx, got_x,
    part_x, part_q, sum_v, zs, zr, full_v,
    bt, st, rt, s2, r2, sgb, rgb,
    sret, ret,
    ld_sem, lx_sem, xs_sem, xr_sem, ds_sem, dr_sem, rs_sem, rr_sem, ws_sem, wr_sem,
    ps_sem, pr_sem, zs_sem, zr_sem, gs_sem, gr_sem, fs_sem, fr_sem,
    a1s_sem, a1r_sem, a2s_sem, a2r_sem, bs_sem, br_sem,
):
    NX, NZH, NAD = geo
    NF = NX * NX
    NZ = NZH * NAD
    NT = 2 * NZH
    tokens = xv.shape[1]
    fw = av.shape[2]
    nd, rank = av.shape[0], av.shape[1]
    vw = bv.shape[2]
    wk = wg.shape[1]
    slots = nd * CAPD
    half = fw // 2
    rc = rank // NF

    fi = lax.axis_index("fsdp")
    ti = lax.axis_index("tp")
    ai = lax.axis_index("ad")
    yi, xi = lax.div(fi, NX), lax.rem(fi, NX)
    zh, core = lax.div(ti, 2), lax.rem(ti, 2)
    z = zh * NAD + ai
    sgn = 1 - 2 * core
    other = 1 - core

    def zdev(k):
        zz = lax.rem(z + k + NZ, NZ)
        return lax.div(zz, NAD), lax.rem(zz, NAD)

    def near(k):
        return lax.rem(ai + k + NAD, NAD)

    def fpeer(jy, jx):
        return lax.rem(yi + jy + NX, NX) * NX + lax.rem(xi + jx + NX, NX)

    def hrow(j):
        return lax.rem(zh + j + NZH, NZH)

    def hpeer(j):
        return {"tp": hrow(j) * 2 + core}

    partner = {"tp": zh * 2 + other}

    ks = [0, (NAD // 2) * sgn]
    for m in (2, 3, 1):
        ks += [m, -m]
    groups = NAD // 2
    foff = [(j // NX, j % NX) for j in range(1, NF)]

    load_dy = pltpu.make_async_copy(dy_hbm, dyv, ld_sem.at[0])
    load_up = pltpu.make_async_copy(up_hbm, bv, ld_sem.at[1])
    load_down = pltpu.make_async_copy(down_hbm, av, ld_sem.at[2])
    load_w = pltpu.make_async_copy(w_hbm, wg.at[fi], ld_sem.at[3])
    load_dy.start()
    load_x = []
    for n in range(NT):
        blk = hrow((0, 1, -1, 2)[n // 2]) * 2 + (core if n % 2 == 0 else other)
        load_x.append((blk, n))
    load_x = load_x[0::2] + load_x[1::2]
    load_x = [
        pltpu.make_async_copy(
            x_hbm.at[:, pl.ds(pl.multiple_of(blk * fw, fw), fw)], xv.at[blk], lx_sem.at[n])
        for blk, n in load_x
    ]
    for c in load_x[:3]:
        c.start()
    load_up.start()
    load_down.start()
    load_w.start()
    for c in load_x[3:]:
        c.start()

    barrier = pltpu.get_barrier_semaphore()
    count = 0

    def greet(device):
        pl.semaphore_signal(barrier, inc=1, device_id=device, device_id_type=MESH)

    for j in (1, -1):
        greet(hpeer(j))
        count += 1
    for k in ks[1:] + [-ks[1]]:
        hh, aa = zdev(k)
        greet({"tp": hh * 2 + core, "ad": aa})
        count += 1
    for j in range(1, NAD):
        greet({"ad": lax.rem(ai + j, NAD)})
        count += 1
    for jy, jx in foff:
        greet({"fsdp": fpeer(jy, jx)})
        count += 1
    greet(partner)
    count += 1

    nall = nd * NAD
    dom_row = dom_ref[...].astype(F32)
    ti0 = lax.broadcasted_iota(jnp.int32, (tokens, tokens), 0)
    ti1 = lax.broadcasted_iota(jnp.int32, (tokens, tokens), 1)
    oh_r = jnp.where(
        dom_row == lax.broadcasted_iota(jnp.int32, (nall, tokens), 0).astype(F32), 1.0, 0.0
    )
    before_r = dot(oh_r.astype(BF16), jnp.where(ti0 < ti1, 1.0, 0.0).astype(BF16))
    place_r = dom_row * float(CAPD) + jnp.sum(before_r * oh_r, axis=0, keepdims=True)

    def pick(dest):
        rows = lax.broadcasted_iota(jnp.int32, (slots, tokens), 0) + dest * slots
        return jnp.where(rows.astype(F32) == place_r, 1.0, 0.0).astype(BF16)

    pending = []

    def go(copy):
        copy.start()
        pending.append(copy)

    load_dy.wait()
    dy_own = dyv[...]
    for i, k in enumerate(ks):
        out = dot(pick(near(k)), dy_own).astype(BF16)
        if i == 0:
            got_dy[0] = out
        else:
            sdy[i] = out
    for c in load_x[:3]:
        c.wait()

    def packed(k):
        hh, aa = zdev(k)
        return dot(pick(aa), xv[hh * 2 + core]).astype(BF16)

    def x_send(i):
        hh, aa = zdev(ks[i])
        go(remote(sx.at[i], got_x.at[i], xs_sem.at[i], xr_sem.at[i],
                  {"tp": hh * 2 + core, "ad": aa}))

    sx[1] = packed(ks[1])
    pl.semaphore_wait(barrier, count)

    for i in range(1, NAD):
        go(remote(sdy.at[i], got_dy.at[i], ds_sem.at[i], dr_sem.at[i], {"ad": near(ks[i])}))
    x_send(1)
    for i in range(2, 4):
        sx[i] = packed(ks[i])
    for i in range(2, 4):
        x_send(i)
    for n, (jy, jx) in enumerate(foff):
        go(remote(w_hbm, wg.at[fi], ws_sem.at[n], wr_sem.at[n], {"fsdp": fpeer(jy, jx)}))
    for i in range(4, EARLY):
        sx[i] = packed(ks[i])
        x_send(i)

    rowdom = lax.broadcasted_iota(jnp.int32, (NAD, slots, rank), 1)

    def own_rows(d, n):
        return (rowdom[:n] >= d * CAPD) & (rowdom[:n] < (d + 1) * CAPD)

    def wait_recv(dst, sem, device):
        remote(dst, dst, sem, sem, device).wait_recv()

    def partial(rows, weight, n):
        acc = jnp.zeros((n, slots, rank), F32)
        for d in range(nd):
            acc = acc + jnp.where(
                own_rows(d, n), dot_nt(rows, weight[d]).reshape(n, slots, rank), 0.0
            )
        return acc

    def share(which, g, value):
        part_x[which, 0, g] = value[0]
        part_x[which, 1, g] = value[1]
        go(remote(part_x.at[which, other, g], part_q.at[which, g],
                  ps_sem.at[which, g], pr_sem.at[which, g], partner))

    def merge(which, g):
        wait_recv(part_q.at[which, g], pr_sem.at[which, g], partner)
        sum_v[which, g] = part_x[which, core, g] + part_q[which, g]

    def chunk(j):
        return hrow(j) * 2 + core

    ring = [[remote(zs.at[w, n], zr.at[w, n], zs_sem.at[w, n], zr_sem.at[w, n], hpeer(to))
             for n, to in enumerate((sgn, sgn, -sgn))] for w in range(2)]
    spread = [[remote(full_v.at[w, chunk(j)], full_v.at[w, chunk(j)], gs_sem.at[w, n],
                      gr_sem.at[w, n], hpeer(to))
               for n, (j, to) in enumerate(((0, sgn), (0, -sgn), (-sgn, sgn)))] for w in range(2)]
    across = [[remote(full_v.at[w, chunk(j)], full_v.at[w, chunk(j)], fs_sem.at[w, n],
                      fr_sem.at[w, n], partner)
               for n, j in enumerate((0, -sgn, sgn, 2))] for w in range(2)]
    for w in range(2):
        pending.extend(ring[w] + spread[w] + across[w])

    def ring_first(which):
        zs[which, 0] = sum_v[which, hrow(2)].astype(BF16)
        ring[which][0].start()

    def ring_side(which):
        zs[which, 2] = sum_v[which, hrow(-sgn)].astype(BF16)
        ring[which][2].start()

    def ring_mid(which):
        wait_recv(zr.at[which, 0], zr_sem.at[which, 0], hpeer(-sgn))
        zs[which, 1] = (sum_v[which, hrow(sgn)] + zr[which, 0].astype(F32)).astype(BF16)
        ring[which][1].start()

    def ring_close(which, scale):
        wait_recv(zr.at[which, 2], zr_sem.at[which, 2], hpeer(sgn))
        wait_recv(zr.at[which, 1], zr_sem.at[which, 1], hpeer(-sgn))
        total = sum_v[which, zh] + zr[which, 1].astype(F32) + zr[which, 2].astype(F32)
        full_v[which, chunk(0)] = (total * scale).astype(BF16)
        spread[which][0].start()
        spread[which][1].start()
        across[which][0].start()

    def gather_mid(which):
        wait_recv(full_v.at[which, chunk(-sgn)], gr_sem.at[which, 0], hpeer(-sgn))
        spread[which][2].start()
        across[which][1].start()

    def gather_side(which):
        wait_recv(full_v.at[which, chunk(sgn)], gr_sem.at[which, 1], hpeer(sgn))
        across[which][2].start()

    def gather_close(which):
        wait_recv(full_v.at[which, chunk(2)], gr_sem.at[which, 2], hpeer(-sgn))
        across[which][3].start()

    def gather_done(which):
        for n, j in enumerate((0, sgn, -sgn, 2)):
            wait_recv(full_v.at[which, hrow(j) * 2 + other], fr_sem.at[which, n], partner)

    def at_row(g, j, step):
        @pl.when(hrow(j) == g)
        def _():
            step()

    def open_row(g):
        merge(1, g)
        at_row(g, 2, lambda: ring_first(1))
        at_row(g, -sgn, lambda: ring_side(1))

    def mid_row(g):
        at_row(g, sgn, lambda: ring_mid(1))

    def close_row(g):
        at_row(g, 0, lambda: ring_close(1, 1.0))

    def spread_row(g):
        at_row(g, -sgn, lambda: gather_mid(1))
        at_row(g, sgn, lambda: gather_side(1))

    def end_row(g):
        at_row(g, 2, lambda: gather_close(1))

    load_up.wait()
    for i in range(1, NAD):
        wait_recv(got_dy.at[i], dr_sem.at[i], {"ad": near(-ks[i])})
    value = partial(got_dy[...].reshape(NAD * slots, vw), bv, NAD)
    for g in range(groups):
        share(0, g, value[2 * g:2 * g + 2])
    for i in range(max(4, EARLY), NAD):
        sx[i] = packed(ks[i])
    for g in range(groups):
        merge(0, g)
    ring_first(0)
    ring_side(0)
    for i in range(max(4, EARLY), NAD):
        x_send(i)
    got_x[0] = packed(0)

    load_down.wait()

    def hidden_group(g):
        for i in (2 * g, 2 * g + 1):
            if i > 0:
                hh, aa = zdev(-ks[i])
                wait_recv(got_x.at[i], xr_sem.at[i], {"tp": hh * 2 + core, "ad": aa})
        share(1, g, partial(got_x[2 * g:2 * g + 2].reshape(2 * slots, fw), av, 2))

    per = NF // NT

    def base_step(n, _):
        rows = wg[pl.ds(n * per, per)].reshape(per * wk, vw)
        base_v[...] = base_v[...] + dot(xv[n], rows)
        return 0

    def base():
        for c in load_x[3:]:
            c.wait()
        load_w.wait()
        for n, (jy, jx) in enumerate(foff):
            src = fpeer(-jy, -jx)
            wait_recv(wg.at[src], wr_sem.at[n], {"fsdp": src})
        base_v[...] = jnp.zeros_like(base_v)
        lax.fori_loop(0, NT, base_step, 0)

    lane = lax.broadcasted_iota(jnp.int32, (rank, NAD * slots), 1).astype(F32)
    lane = lane - float(slots) * jnp.floor((lane + 0.5) / float(slots))

    def lane_dom(d):
        return (lane >= float(d * CAPD)) & (lane < float((d + 1) * CAPD))

    def prepare_a():
        back_t = full_v[0].reshape(NAD * slots, rank).astype(F32).T
        for d in range(nd):
            bt[d] = jnp.where(lane_dom(d), back_t, 0.0).astype(BF16)

    pairs = nd // 2
    line = (xi, yi)

    def axis_peer(h, j):
        if h == 0:
            return {"fsdp": fpeer(0, j)}
        return {"fsdp": fpeer(j, 0)}

    def part_a(h, p):
        def one(e, _):
            res = dot(
                bt[p * 2 + e], got_x[:, :, h * half:(h + 1) * half].reshape(NAD * slots, half)
            ).astype(BF16).reshape(NF, rc, half)
            for f in range(NF):
                yx = (f // NX, f % NX)
                st[h, p, yx[1 - h], yx[h], e] = res[f]
            return 0

        lax.fori_loop(0, 2, one, 0)
        for j in range(1, NX):
            go(remote(st.at[h, p, lax.rem(line[h] + j, NX)], rt.at[h, p, j],
                      a1s_sem.at[h, p, j], a1r_sem.at[h, p, j], axis_peer(h, j)))

    def fold_a(h, p):
        for j in range(1, NX):
            wait_recv(rt.at[h, p, j], a1r_sem.at[h, p, j], axis_peer(h, -j))
        for i in range(NX):
            at = lax.rem(line[1 - h] + i, NX)
            tot = st[h, p, line[h], at].astype(F32)
            for j in range(1, NX):
                tot = tot + rt[h, p, j, at].astype(F32)
            s2[h, p, i] = tot
        for i in range(1, NX):
            go(remote(s2.at[h, p, i], r2.at[h, p, i], a2s_sem.at[h, p, i], a2r_sem.at[h, p, i],
                      axis_peer(1 - h, i)))

    pieces = [(h, p) for p in range(pairs) for h in range(2)]
    hidden_group(0)
    open_row(0)
    hidden_group(1)
    open_row(1)
    ring_mid(0)
    hidden_group(2)
    open_row(2)
    hidden_group(3)
    open_row(3)
    ring_close(0, adapter_scale)
    mid_row(0)
    mid_row(1)
    mid_row(2)
    mid_row(3)
    gather_mid(0)
    gather_side(0)
    base()
    close_row(0)
    close_row(1)
    close_row(2)
    close_row(3)
    gather_close(0)
    gather_done(0)
    prepare_a()
    part_a(*pieces[0])
    part_a(*pieces[1])
    spread_row(0)
    spread_row(1)
    spread_row(2)
    spread_row(3)
    part_a(*pieces[2])
    part_a(*pieces[3])
    fold_a(*pieces[0])
    fold_a(*pieces[1])
    end_row(0)
    end_row(1)
    end_row(2)
    end_row(3)
    gather_done(1)

    hid = full_v[1].astype(F32)
    acc = jnp.zeros((NAD * slots, vw), F32)
    for d in range(nd):
        mine = jnp.where(own_rows(d, NAD), hid, 0.0).astype(BF16).reshape(NAD * slots, rank)
        acc = acc + dot(mine, bv[d])
    sret[...] = (adapter_scale * acc).astype(BF16).reshape(NAD, slots, vw)
    hid_t = hid.reshape(NAD * slots, rank).T
    for i in range(1, NAD):
        go(remote(sret.at[i], ret.at[i], rs_sem.at[i], rr_sem.at[i], {"ad": near(-ks[i])}))
    ret[0] = sret[0]
    rows_dy = got_dy[...].reshape(NAD * slots, vw)
    for d in range(nd):
        mine = jnp.where(lane_dom(d), hid_t, 0.0).astype(BF16)
        res = (adapter_scale * dot(mine, rows_dy)).astype(BF16).reshape(NF, rc, vw)
        for f in range(NF):
            sgb[f, d] = res[f]
    for n, (jy, jx) in enumerate(foff):
        dst = fpeer(jy, jx)
        go(remote(sgb.at[dst], rgb.at[n + 1], bs_sem.at[n], br_sem.at[n], {"fsdp": dst}))
    fold_a(*pieces[2])
    fold_a(*pieces[3])

    place_c = jnp.broadcast_to(place_r, (128, tokens)).T[:, 0:1]
    col = lax.broadcasted_iota(jnp.int32, (1, NAD * slots), 1)
    ident = jnp.zeros((1, NAD * slots), jnp.int32)
    for i, k in enumerate(ks):
        inside = (col >= i * slots) & (col < (i + 1) * slots)
        ident = jnp.where(inside, col + (near(k) - i) * slots, ident)
    unpick = jnp.where(ident.astype(F32) == place_c, 1.0, 0.0).astype(BF16)
    for i in range(1, NAD):
        wait_recv(ret.at[i], rr_sem.at[i], {"ad": near(ks[i])})
    y_ref[...] = (base_v[...] + dot(unpick, ret[...].reshape(NAD * slots, vw))).astype(BF16)

    tot = sgb[fi].astype(F32)
    for n, (jy, jx) in enumerate(foff):
        wait_recv(rgb.at[n + 1], br_sem.at[n], {"fsdp": fpeer(-jy, -jx)})
        tot = tot + rgb[n + 1].astype(F32)
    gb_ref[...] = tot
    for h, p in pieces:
        tot = s2[h, p, 0]
        for i in range(1, NX):
            wait_recv(r2.at[h, p, i], a2r_sem.at[h, p, i], axis_peer(1 - h, -i))
            tot = tot + r2[h, p, i]
        ga_ref[2 * p:2 * p + 2, :, h * half:(h + 1) * half] = tot

    for copy in pending:
        copy.wait_send()


def finish(y_in, ga_in, gb_in, y_ref, ga_ref, gb_ref, yv, gav, gbv, in_sem, out_sem):
    stages = ((y_in, yv, y_ref), (ga_in, gav, ga_ref), (gb_in, gbv, gb_ref))
    into = [pltpu.make_async_copy(a, v, in_sem.at[n]) for n, (a, v, _) in enumerate(stages)]
    out = [pltpu.make_async_copy(v, o, out_sem.at[n]) for n, (_, v, o) in enumerate(stages)]
    for c in into:
        c.start()
    for c, o in zip(into, out):
        c.wait()
        o.start()
    for o in out:
        o.wait()


def body(geo, x, w, down, up, dy, domain):
    NX, NZH, NAD = geo
    NF = NX * NX
    NT = 2 * NZH
    tokens = x.shape[0]
    nd, rank, fw = down.shape
    vw = up.shape[2]
    slots = nd * CAPD
    half = fw // 2
    rc = rank // NF
    pairs = nd // 2
    V, D = pltpu.VMEM, pltpu.SemaphoreType.DMA
    scratch = [
        V((NT, tokens, fw), BF16), V((NF,) + w.shape, BF16), V(down.shape, BF16),
        V(up.shape, BF16), V(dy.shape, BF16), V((tokens, vw), F32),
        V((NAD, slots, vw), BF16), V((NAD, slots, vw), BF16),
        V((NAD, slots, fw), BF16), V((NAD, slots, fw), BF16),
        V((2, 2, NZH, slots, rank), F32), V((2, NZH, slots, rank), F32),
        V((2, NZH, slots, rank), F32),
        V((2, 3, slots, rank), BF16), V((2, 3, slots, rank), BF16),
        V((2, NAD, slots, rank), BF16),
        V((nd, rank, NAD * slots), BF16),
        V((2, pairs, NX, NX, 2, rc, half), BF16), V((2, pairs, NX, NX, 2, rc, half), BF16),
        V((2, pairs, NX, 2, rc, half), F32), V((2, pairs, NX, 2, rc, half), F32),
        V((NF, nd, rc, vw), BF16), V((NF, nd, rc, vw), BF16),
        V((NAD, slots, vw), BF16), V((NAD, slots, vw), BF16),
        D((4,)), D((NT,)),
        D((NAD,)), D((NAD,)), D((NAD,)), D((NAD,)), D((NAD,)), D((NAD,)), D((NF,)), D((NF,)),
        D((2, NZH)), D((2, NZH)), D((2, 3)), D((2, 3)), D((2, 3)), D((2, 3)), D((2, 4)), D((2, 4)),
        D((2, pairs, NX)), D((2, pairs, NX)), D((2, pairs, NX)), D((2, pairs, NX)),
        D((NF,)), D((NF,)),
    ]
    vm = pl.BlockSpec(memory_space=pltpu.VMEM)
    hbm = pl.BlockSpec(memory_space=pltpu.HBM)
    shapes = (
        jax.ShapeDtypeStruct((tokens, vw), BF16),
        jax.ShapeDtypeStruct((nd, rc, fw), F32),
        jax.ShapeDtypeStruct((nd, rc, vw), F32),
    )
    results = pl.pallas_call(
        functools.partial(kernel, geo),
        out_shape=shapes,
        in_specs=[vm, hbm, hbm, hbm, hbm, hbm],
        out_specs=(vm, vm, vm),
        scratch_shapes=scratch,
        compiler_params=pltpu.CompilerParams(
            collective_id=0, has_side_effects=True, vmem_limit_bytes=VLIM * 1024 * 1024
        ),
        name="adapters",
    )(domain.reshape(1, tokens), x, w, down, up, dy)
    return tuple(
        pl.pallas_call(
            finish, out_shape=shapes, in_specs=[hbm] * 3, out_specs=(hbm,) * 3,
            scratch_shapes=[V(t.shape, t.dtype) for t in shapes] + [D((3,)), D((3,))],
            compiler_params=pltpu.CompilerParams(vmem_limit_bytes=VLIM * 1024 * 1024),
            name="finish",
        )(*results)
    )


def geometry(mesh):
    return (4, mesh.shape["tp"] // 2, mesh.shape["ad"])


def solution(mesh):
    placed = (
        P(("fsdp", "ad"), None),
        P("fsdp", "tp"),
        P("ad", None, "tp"),
        P("ad", None, "tp"),
        P(("fsdp", "ad"), "tp"),
        P(("fsdp", "ad"), None),
    )
    return jax.shard_map(
        functools.partial(body, geometry(mesh)),
        mesh=mesh,
        in_specs=placed,
        out_specs=(P(("fsdp", "ad"), "tp"), P("ad", "fsdp", "tp"), P("ad", "fsdp", "tp")),
        check_vma=False,
    )
```

```python
import functools

import jax
import jax.numpy as jnp
from jax import lax
from jax.experimental import pallas as pl
from jax.experimental.pallas import tpu as pltpu
from jax.sharding import PartitionSpec as P

CAPD = 12
adapter_scale = 0.5
EARLY = 4
VLIM = 63
MESH = pl.DeviceIdType.MESH
F32 = jnp.float32
BF16 = jnp.bfloat16


def remote(src, dst, send_sem, recv_sem, device):
    return pltpu.make_async_remote_copy(
        src_ref=src, dst_ref=dst, send_sem=send_sem, recv_sem=recv_sem,
        device_id=device, device_id_type=MESH,
    )


def dot(a, b):
    return jnp.dot(a, b, preferred_element_type=F32)


def dot_nt(a, b):
    return lax.dot_general(a, b, (((1,), (1,)), ((), ())), preferred_element_type=F32)


def kernel(
    geo,
    dom_ref, x_hbm, w_hbm, down_hbm, up_hbm, dy_hbm,
    y_ref, ga_ref, gb_ref,
    xv, wg, av, bv, dyv, base_v,
    sdy, got_dy, sx, got_x,
    part_x, part_q, sum_v, zs, zr, full_v,
    bt, st, rt, s2, r2, sgb, rgb,
    sret, ret,
    ld_sem, lx_sem, xs_sem, xr_sem, ds_sem, dr_sem, rs_sem, rr_sem, ws_sem, wr_sem,
    ps_sem, pr_sem, zs_sem, zr_sem, gs_sem, gr_sem, fs_sem, fr_sem,
    a1s_sem, a1r_sem, a2s_sem, a2r_sem, bs_sem, br_sem,
):
    NX, NZH, NAD = geo
    NF = NX * NX
    NZ = NZH * NAD
    NT = 2 * NZH
    tokens = xv.shape[1]
    fw = av.shape[2]
    nd, rank = av.shape[0], av.shape[1]
    vw = bv.shape[2]
    wk = wg.shape[1]
    slots = nd * CAPD
    half = fw // 2
    rc = rank // NF

    fi = lax.axis_index("fsdp")
    ti = lax.axis_index("tp")
    ai = lax.axis_index("ad")
    yi, xi = lax.div(fi, NX), lax.rem(fi, NX)
    zh, core = lax.div(ti, 2), lax.rem(ti, 2)
    z = zh * NAD + ai
    sgn = 1 - 2 * core
    other = 1 - core

    def zdev(k):
        zz = lax.rem(z + k + NZ, NZ)
        return lax.div(zz, NAD), lax.rem(zz, NAD)

    def near(k):
        return lax.rem(ai + k + NAD, NAD)

    def fpeer(jy, jx):
        return lax.rem(yi + jy + NX, NX) * NX + lax.rem(xi + jx + NX, NX)

    def hrow(j):
        return lax.rem(zh + j + NZH, NZH)

    def hpeer(j):
        return {"tp": hrow(j) * 2 + core}

    partner = {"tp": zh * 2 + other}

    ks = [0, (NAD // 2) * sgn]
    for m in (2, 3, 1):
        ks += [m, -m]
    groups = NAD // 2
    foff = [(j // NX, j % NX) for j in range(1, NF)]

    load_dy = pltpu.make_async_copy(dy_hbm, dyv, ld_sem.at[0])
    load_up = pltpu.make_async_copy(up_hbm, bv, ld_sem.at[1])
    load_down = pltpu.make_async_copy(down_hbm, av, ld_sem.at[2])
    load_w = pltpu.make_async_copy(w_hbm, wg.at[fi], ld_sem.at[3])
    load_dy.start()
    load_x = []
    for n in range(NT):
        blk = hrow((0, 1, -1, 2)[n // 2]) * 2 + (core if n % 2 == 0 else other)
        load_x.append((blk, n))
    load_x = load_x[0::2] + load_x[1::2]
    load_x = [
        pltpu.make_async_copy(
            x_hbm.at[:, pl.ds(pl.multiple_of(blk * fw, fw), fw)], xv.at[blk], lx_sem.at[n])
        for blk, n in load_x
    ]
    for c in load_x[:3]:
        c.start()
    load_up.start()
    load_down.start()
    load_w.start()
    for c in load_x[3:]:
        c.start()

    barrier = pltpu.get_barrier_semaphore()
    count = 0

    def greet(device):
        pl.semaphore_signal(barrier, inc=1, device_id=device, device_id_type=MESH)

    for j in (1, -1):
        greet(hpeer(j))
        count += 1
    for k in ks[1:] + [-ks[1]]:
        hh, aa = zdev(k)
        greet({"tp": hh * 2 + core, "ad": aa})
        count += 1
    for j in range(1, NAD):
        greet({"ad": lax.rem(ai + j, NAD)})
        count += 1
    for jy, jx in foff:
        greet({"fsdp": fpeer(jy, jx)})
        count += 1
    greet(partner)
    count += 1

    nall = nd * NAD
    dom_row = dom_ref[...].astype(F32)
    ti0 = lax.broadcasted_iota(jnp.int32, (tokens, tokens), 0)
    ti1 = lax.broadcasted_iota(jnp.int32, (tokens, tokens), 1)
    oh_r = jnp.where(
        dom_row == lax.broadcasted_iota(jnp.int32, (nall, tokens), 0).astype(F32), 1.0, 0.0
    )
    before_r = dot(oh_r.astype(BF16), jnp.where(ti0 < ti1, 1.0, 0.0).astype(BF16))
    place_r = dom_row * float(CAPD) + jnp.sum(before_r * oh_r, axis=0, keepdims=True)

    def pick(dest):
        rows = lax.broadcasted_iota(jnp.int32, (slots, tokens), 0) + dest * slots
        return jnp.where(rows.astype(F32) == place_r, 1.0, 0.0).astype(BF16)

    pending = []

    def go(copy):
        copy.start()
        pending.append(copy)

    load_dy.wait()
    dy_own = dyv[...]
    for i, k in enumerate(ks):
        out = dot(pick(near(k)), dy_own).astype(BF16)
        if i == 0:
            got_dy[0] = out
        else:
            sdy[i] = out
    for c in load_x[:3]:
        c.wait()

    def packed(k):
        hh, aa = zdev(k)
        return dot(pick(aa), xv[hh * 2 + core]).astype(BF16)

    def x_send(i):
        hh, aa = zdev(ks[i])
        go(remote(sx.at[i], got_x.at[i], xs_sem.at[i], xr_sem.at[i],
                  {"tp": hh * 2 + core, "ad": aa}))

    sx[1] = packed(ks[1])
    pl.semaphore_wait(barrier, count)

    for i in range(1, NAD):
        go(remote(sdy.at[i], got_dy.at[i], ds_sem.at[i], dr_sem.at[i], {"ad": near(ks[i])}))
    x_send(1)
    for i in range(2, 4):
        sx[i] = packed(ks[i])
    for i in range(2, 4):
        x_send(i)
    for n, (jy, jx) in enumerate(foff):
        go(remote(w_hbm, wg.at[fi], ws_sem.at[n], wr_sem.at[n], {"fsdp": fpeer(jy, jx)}))
    for i in range(4, EARLY):
        sx[i] = packed(ks[i])
        x_send(i)

    rowdom = lax.broadcasted_iota(jnp.int32, (NAD, slots, rank), 1)

    def own_rows(d, n):
        return (rowdom[:n] >= d * CAPD) & (rowdom[:n] < (d + 1) * CAPD)

    def wait_recv(dst, sem, device):
        remote(dst, dst, sem, sem, device).wait_recv()

    def partial(rows, weight, n):
        acc = jnp.zeros((n, slots, rank), F32)
        for d in range(nd):
            acc = acc + jnp.where(
                own_rows(d, n), dot_nt(rows, weight[d]).reshape(n, slots, rank), 0.0
            )
        return acc

    def share(which, g, value):
        part_x[which, 0, g] = value[0]
        part_x[which, 1, g] = value[1]
        go(remote(part_x.at[which, other, g], part_q.at[which, g],
                  ps_sem.at[which, g], pr_sem.at[which, g], partner))

    def merge(which, g):
        wait_recv(part_q.at[which, g], pr_sem.at[which, g], partner)
        sum_v[which, g] = part_x[which, core, g] + part_q[which, g]

    def chunk(j):
        return hrow(j) * 2 + core

    ring = [[remote(zs.at[w, n], zr.at[w, n], zs_sem.at[w, n], zr_sem.at[w, n], hpeer(to))
             for n, to in enumerate((sgn, sgn, -sgn))] for w in range(2)]
    spread = [[remote(full_v.at[w, chunk(j)], full_v.at[w, chunk(j)], gs_sem.at[w, n],
                      gr_sem.at[w, n], hpeer(to))
               for n, (j, to) in enumerate(((0, sgn), (0, -sgn), (-sgn, sgn)))] for w in range(2)]
    across = [[remote(full_v.at[w, chunk(j)], full_v.at[w, chunk(j)], fs_sem.at[w, n],
                      fr_sem.at[w, n], partner)
               for n, j in enumerate((0, -sgn, sgn, 2))] for w in range(2)]
    for w in range(2):
        pending.extend(ring[w] + spread[w] + across[w])

    def ring_first(which):
        zs[which, 0] = sum_v[which, hrow(2)].astype(BF16)
        ring[which][0].start()

    def ring_side(which):
        zs[which, 2] = sum_v[which, hrow(-sgn)].astype(BF16)
        ring[which][2].start()

    def ring_mid(which):
        wait_recv(zr.at[which, 0], zr_sem.at[which, 0], hpeer(-sgn))
        zs[which, 1] = (sum_v[which, hrow(sgn)] + zr[which, 0].astype(F32)).astype(BF16)
        ring[which][1].start()

    def ring_close(which, scale):
        wait_recv(zr.at[which, 2], zr_sem.at[which, 2], hpeer(sgn))
        wait_recv(zr.at[which, 1], zr_sem.at[which, 1], hpeer(-sgn))
        total = sum_v[which, zh] + zr[which, 1].astype(F32) + zr[which, 2].astype(F32)
        full_v[which, chunk(0)] = (total * scale).astype(BF16)
        spread[which][0].start()
        spread[which][1].start()
        across[which][0].start()

    def gather_mid(which):
        wait_recv(full_v.at[which, chunk(-sgn)], gr_sem.at[which, 0], hpeer(-sgn))
        spread[which][2].start()
        across[which][1].start()

    def gather_side(which):
        wait_recv(full_v.at[which, chunk(sgn)], gr_sem.at[which, 1], hpeer(sgn))
        across[which][2].start()

    def gather_close(which):
        wait_recv(full_v.at[which, chunk(2)], gr_sem.at[which, 2], hpeer(-sgn))
        across[which][3].start()

    def gather_done(which):
        for n, j in enumerate((0, sgn, -sgn, 2)):
            wait_recv(full_v.at[which, hrow(j) * 2 + other], fr_sem.at[which, n], partner)

    def at_row(g, j, step):
        @pl.when(hrow(j) == g)
        def _():
            step()

    def open_row(g):
        merge(1, g)
        at_row(g, 2, lambda: ring_first(1))
        at_row(g, -sgn, lambda: ring_side(1))

    def mid_row(g):
        at_row(g, sgn, lambda: ring_mid(1))

    def close_row(g):
        at_row(g, 0, lambda: ring_close(1, 1.0))

    def spread_row(g):
        at_row(g, -sgn, lambda: gather_mid(1))
        at_row(g, sgn, lambda: gather_side(1))

    def end_row(g):
        at_row(g, 2, lambda: gather_close(1))

    load_up.wait()
    for i in range(1, NAD):
        wait_recv(got_dy.at[i], dr_sem.at[i], {"ad": near(-ks[i])})
    value = partial(got_dy[...].reshape(NAD * slots, vw), bv, NAD)
    for g in range(groups):
        share(0, g, value[2 * g:2 * g + 2])
    for i in range(max(4, EARLY), NAD):
        sx[i] = packed(ks[i])
    for g in range(groups):
        merge(0, g)
    ring_first(0)
    ring_side(0)
    for i in range(max(4, EARLY), NAD):
        x_send(i)
    got_x[0] = packed(0)

    load_down.wait()

    def hidden_group(g):
        for i in (2 * g, 2 * g + 1):
            if i > 0:
                hh, aa = zdev(-ks[i])
                wait_recv(got_x.at[i], xr_sem.at[i], {"tp": hh * 2 + core, "ad": aa})
        share(1, g, partial(got_x[2 * g:2 * g + 2].reshape(2 * slots, fw), av, 2))

    per = NF // NT

    def base_step(n, _):
        rows = wg[pl.ds(n * per, per)].reshape(per * wk, vw)
        base_v[...] = base_v[...] + dot(xv[n], rows)
        return 0

    def base():
        for c in load_x[3:]:
            c.wait()
        load_w.wait()
        for n, (jy, jx) in enumerate(foff):
            src = fpeer(-jy, -jx)
            wait_recv(wg.at[src], wr_sem.at[n], {"fsdp": src})
        base_v[...] = jnp.zeros_like(base_v)
        lax.fori_loop(0, NT, base_step, 0)

    lane = lax.broadcasted_iota(jnp.int32, (rank, NAD * slots), 1).astype(F32)
    lane = lane - float(slots) * jnp.floor((lane + 0.5) / float(slots))

    def lane_dom(d):
        return (lane >= float(d * CAPD)) & (lane < float((d + 1) * CAPD))

    def prepare_a():
        back_t = full_v[0].reshape(NAD * slots, rank).astype(F32).T
        for d in range(nd):
            bt[d] = jnp.where(lane_dom(d), back_t, 0.0).astype(BF16)

    pairs = nd // 2
    line = (xi, yi)

    def axis_peer(h, j):
        if h == 0:
            return {"fsdp": fpeer(0, j)}
        return {"fsdp": fpeer(j, 0)}

    def part_a(h, p):
        def one(e, _):
            res = dot(
                bt[p * 2 + e], got_x[:, :, h * half:(h + 1) * half].reshape(NAD * slots, half)
            ).astype(BF16).reshape(NF, rc, half)
            for f in range(NF):
                yx = (f // NX, f % NX)
                st[h, p, yx[1 - h], yx[h], e] = res[f]
            return 0

        lax.fori_loop(0, 2, one, 0)
        for j in range(1, NX):
            go(remote(st.at[h, p, lax.rem(line[h] + j, NX)], rt.at[h, p, j],
                      a1s_sem.at[h, p, j], a1r_sem.at[h, p, j], axis_peer(h, j)))

    def fold_a(h, p):
        for j in range(1, NX):
            wait_recv(rt.at[h, p, j], a1r_sem.at[h, p, j], axis_peer(h, -j))
        for i in range(NX):
            at = lax.rem(line[1 - h] + i, NX)
            tot = st[h, p, line[h], at].astype(F32)
            for j in range(1, NX):
                tot = tot + rt[h, p, j, at].astype(F32)
            s2[h, p, i] = tot
        for i in range(1, NX):
            go(remote(s2.at[h, p, i], r2.at[h, p, i], a2s_sem.at[h, p, i], a2r_sem.at[h, p, i],
                      axis_peer(1 - h, i)))

    pieces = [(h, p) for p in range(pairs) for h in range(2)]
    hidden_group(0)
    open_row(0)
    hidden_group(1)
    open_row(1)
    ring_mid(0)
    hidden_group(2)
    open_row(2)
    hidden_group(3)
    open_row(3)
    ring_close(0, adapter_scale)
    mid_row(0)
    mid_row(1)
    mid_row(2)
    mid_row(3)
    gather_mid(0)
    gather_side(0)
    base()
    close_row(0)
    close_row(1)
    close_row(2)
    close_row(3)
    gather_close(0)
    gather_done(0)
    prepare_a()
    part_a(*pieces[0])
    part_a(*pieces[1])
    spread_row(0)
    spread_row(1)
    spread_row(2)
    spread_row(3)
    part_a(*pieces[2])
    part_a(*pieces[3])
    fold_a(*pieces[0])
    fold_a(*pieces[1])
    end_row(0)
    end_row(1)
    end_row(2)
    end_row(3)
    gather_done(1)

    hid = full_v[1].astype(F32)
    acc = jnp.zeros((NAD * slots, vw), F32)
    for d in range(nd):
        mine = jnp.where(own_rows(d, NAD), hid, 0.0).astype(BF16).reshape(NAD * slots, rank)
        acc = acc + dot(mine, bv[d])
    sret[...] = (adapter_scale * acc).astype(BF16).reshape(NAD, slots, vw)
    hid_t = hid.reshape(NAD * slots, rank).T
    for i in range(1, NAD):
        go(remote(sret.at[i], ret.at[i], rs_sem.at[i], rr_sem.at[i], {"ad": near(-ks[i])}))
    fold_a(*pieces[2])
    fold_a(*pieces[3])
    ret[0] = sret[0]
    rows_dy = got_dy[...].reshape(NAD * slots, vw)
    for d in range(nd):
        mine = jnp.where(lane_dom(d), hid_t, 0.0).astype(BF16)
        res = (adapter_scale * dot(mine, rows_dy)).astype(BF16).reshape(NF, rc, vw)
        for f in range(NF):
            sgb[f, d] = res[f]
    for n, (jy, jx) in enumerate(foff):
        dst = fpeer(jy, jx)
        go(remote(sgb.at[dst], rgb.at[n + 1], bs_sem.at[n], br_sem.at[n], {"fsdp": dst}))

    place_c = jnp.broadcast_to(place_r, (128, tokens)).T[:, 0:1]
    col = lax.broadcasted_iota(jnp.int32, (1, NAD * slots), 1)
    ident = jnp.zeros((1, NAD * slots), jnp.int32)
    for i, k in enumerate(ks):
        inside = (col >= i * slots) & (col < (i + 1) * slots)
        ident = jnp.where(inside, col + (near(k) - i) * slots, ident)
    unpick = jnp.where(ident.astype(F32) == place_c, 1.0, 0.0).astype(BF16)
    for i in range(1, NAD):
        wait_recv(ret.at[i], rr_sem.at[i], {"ad": near(ks[i])})
    y_ref[...] = (base_v[...] + dot(unpick, ret[...].reshape(NAD * slots, vw))).astype(BF16)

    tot = sgb[fi].astype(F32)
    for n, (jy, jx) in enumerate(foff):
        wait_recv(rgb.at[n + 1], br_sem.at[n], {"fsdp": fpeer(-jy, -jx)})
        tot = tot + rgb[n + 1].astype(F32)
    gb_ref[...] = tot
    for h, p in pieces:
        tot = s2[h, p, 0]
        for i in range(1, NX):
            wait_recv(r2.at[h, p, i], a2r_sem.at[h, p, i], axis_peer(1 - h, -i))
            tot = tot + r2[h, p, i]
        ga_ref[2 * p:2 * p + 2, :, h * half:(h + 1) * half] = tot

    for copy in pending:
        copy.wait_send()


def finish(y_in, ga_in, gb_in, y_ref, ga_ref, gb_ref, yv, gav, gbv, in_sem, out_sem):
    stages = ((y_in, yv, y_ref), (ga_in, gav, ga_ref), (gb_in, gbv, gb_ref))
    into = [pltpu.make_async_copy(a, v, in_sem.at[n]) for n, (a, v, _) in enumerate(stages)]
    out = [pltpu.make_async_copy(v, o, out_sem.at[n]) for n, (_, v, o) in enumerate(stages)]
    for c in into:
        c.start()
    for c, o in zip(into, out):
        c.wait()
        o.start()
    for o in out:
        o.wait()


def body(geo, x, w, down, up, dy, domain):
    NX, NZH, NAD = geo
    NF = NX * NX
    NT = 2 * NZH
    tokens = x.shape[0]
    nd, rank, fw = down.shape
    vw = up.shape[2]
    slots = nd * CAPD
    half = fw // 2
    rc = rank // NF
    pairs = nd // 2
    V, D = pltpu.VMEM, pltpu.SemaphoreType.DMA
    scratch = [
        V((NT, tokens, fw), BF16), V((NF,) + w.shape, BF16), V(down.shape, BF16),
        V(up.shape, BF16), V(dy.shape, BF16), V((tokens, vw), F32),
        V((NAD, slots, vw), BF16), V((NAD, slots, vw), BF16),
        V((NAD, slots, fw), BF16), V((NAD, slots, fw), BF16),
        V((2, 2, NZH, slots, rank), F32), V((2, NZH, slots, rank), F32),
        V((2, NZH, slots, rank), F32),
        V((2, 3, slots, rank), BF16), V((2, 3, slots, rank), BF16),
        V((2, NAD, slots, rank), BF16),
        V((nd, rank, NAD * slots), BF16),
        V((2, pairs, NX, NX, 2, rc, half), BF16), V((2, pairs, NX, NX, 2, rc, half), BF16),
        V((2, pairs, NX, 2, rc, half), F32), V((2, pairs, NX, 2, rc, half), F32),
        V((NF, nd, rc, vw), BF16), V((NF, nd, rc, vw), BF16),
        V((NAD, slots, vw), BF16), V((NAD, slots, vw), BF16),
        D((4,)), D((NT,)),
        D((NAD,)), D((NAD,)), D((NAD,)), D((NAD,)), D((NAD,)), D((NAD,)), D((NF,)), D((NF,)),
        D((2, NZH)), D((2, NZH)), D((2, 3)), D((2, 3)), D((2, 3)), D((2, 3)), D((2, 4)), D((2, 4)),
        D((2, pairs, NX)), D((2, pairs, NX)), D((2, pairs, NX)), D((2, pairs, NX)),
        D((NF,)), D((NF,)),
    ]
    vm = pl.BlockSpec(memory_space=pltpu.VMEM)
    hbm = pl.BlockSpec(memory_space=pltpu.HBM)
    shapes = (
        jax.ShapeDtypeStruct((tokens, vw), BF16),
        jax.ShapeDtypeStruct((nd, rc, fw), F32),
        jax.ShapeDtypeStruct((nd, rc, vw), F32),
    )
    results = pl.pallas_call(
        functools.partial(kernel, geo),
        out_shape=shapes,
        in_specs=[vm, hbm, hbm, hbm, hbm, hbm],
        out_specs=(vm, vm, vm),
        scratch_shapes=scratch,
        compiler_params=pltpu.CompilerParams(
            collective_id=0, has_side_effects=True, vmem_limit_bytes=VLIM * 1024 * 1024
        ),
        name="adapters",
    )(domain.reshape(1, tokens), x, w, down, up, dy)
    return tuple(
        pl.pallas_call(
            finish, out_shape=shapes, in_specs=[hbm] * 3, out_specs=(hbm,) * 3,
            scratch_shapes=[V(t.shape, t.dtype) for t in shapes] + [D((3,)), D((3,))],
            compiler_params=pltpu.CompilerParams(vmem_limit_bytes=VLIM * 1024 * 1024),
            name="finish",
        )(*results)
    )


def geometry(mesh):
    return (4, mesh.shape["tp"] // 2, mesh.shape["ad"])


def solution(mesh):
    placed = (
        P(("fsdp", "ad"), None),
        P("fsdp", "tp"),
        P("ad", None, "tp"),
        P("ad", None, "tp"),
        P(("fsdp", "ad"), "tp"),
        P(("fsdp", "ad"), None),
    )
    return jax.shard_map(
        functools.partial(body, geometry(mesh)),
        mesh=mesh,
        in_specs=placed,
        out_specs=(P(("fsdp", "ad"), "tp"), P("ad", "fsdp", "tp"), P("ad", "fsdp", "tp")),
        check_vma=False,
    )
```
